32 devices in a mesh: rep: 1, fsdp: 32 (over z, y, x, core).
Axes of the slice: x: 2, y: 2, z: 4, core: 2. Of those that a mesh axis runs over, the one named last changes fastest.
Arguments:
- tokens: bfloat16 [24576, 4096], P(('rep', 'fsdp')), may hold values from -6 to 6
- cotangent: bfloat16 [24576, 512], P(('rep', 'fsdp')), may hold values from -0.0390625 to 0.0390625
- policy: float32 [4096, 512], P('fsdp'), may hold values from -0.09375 to 0.09375
- anchor: float32 [4096, 512], P('fsdp'), may hold values from -0.09375 to 0.09375
- moment: float32 [4096, 512], P('fsdp'), may hold values from -3 to 3
- second: float32 [4096, 512], P('fsdp'), may hold values from 0.25 to 4
- readout: float32 [512], replicated, may hold values from -6 to 6
- pair_index: int32 [64, 2], P(('rep', 'fsdp')), may hold values from 0 to 127, as said below
- noisy_flags: int32 [64], P(('rep', 'fsdp')), may hold values 0 or 1
Outputs:
- policy_next: float32 [4096, 512], P('fsdp')
- anchor_next: float32 [4096, 512], P('fsdp')
- moment_next: float32 [4096, 512], P('fsdp')
- second_next: float32 [4096, 512], P('fsdp')
- pair_loss: float32 [64], P(('rep', 'fsdp'))
The draws below stay inside these ranges and needn't reach their ends.
Inputs may be any that keep to these rules, and one draw needn't show every extreme that they name: Each of the 128 sequences appears exactly once in pair_index.
All inputs are finite; a program needn't handle non-finite values. No bound on the sum of `noisy_flags` on one device may be relied on, other than what follows from the above.
Results may differ from the reference program's by a relative error of at most 0.0025.
Values may be sent and summed in bfloat16 or wider, within the bound.
A program may use at most 64 MiB of HBM per device.

```python
import math
import jax
import jax.numpy as jnp
from jax import lax

D = 4096
DV = 512
LEN = 192
TOKENS = 24576
NSEQ = 128
PAIRS = 64


def draw_pair_index(key, part):
    shuffled = jax.random.permutation(jax.random.fold_in(key, 11), NSEQ)
    return shuffled.astype(jnp.int32).reshape(PAIRS, 2)


def touch_ends(values, own_key, least, high):
    longest = values.shape.index(max(values.shape))
    spots = []
    for shift in (0, 1):
        where = [jax.random.randint(jax.random.fold_in(own_key, axis), (), 0, length) for axis, length in enumerate(values.shape)]
        where[longest] = (where[longest] + shift) % values.shape[longest]
        spots.append(tuple(where))
    return values.at[spots[0]].set(least).at[spots[1]].set(high)


def strengthened(entries, rng, source, target, parts, factor):
    owner, partner = [(jnp.arange(entries.shape[position]) // (entries.shape[position] // parts)).reshape([-1 if axis == position else 1 for axis in range(entries.ndim)]) for position in (source, target)]
    chosen = jax.random.permutation(rng, parts)[partner]
    strong = (owner == chosen) | (owner == (partner + parts // 2) % parts)
    return jnp.where(strong, factor * entries, entries)


def block_levels(key, dims, cuts, low, top_value):
    def one(axis_at, shards_of):
        heights = jax.random.uniform(jax.random.fold_in(jax.random.fold_in(key, 6), axis_at), (shards_of,), jnp.float32, low / len(cuts), top_value / len(cuts))
        return jnp.repeat(jnp.exp(heights), dims[axis_at] // shards_of).reshape((-1,) + (1,) * (len(dims) - axis_at - 1))

    loudness = one(*cuts[0])
    for cut in cuts[1:]:
        loudness = loudness * one(*cut)
    return loudness


def noise(key, dims, deviation, limit, shards=(), held_as=jnp.bfloat16):
    factor_of = block_levels(key, dims, shards, -0.22, 0.18) if shards else 1.0
    array = jax.random.normal(key, dims, jnp.float32) * deviation * factor_of
    return jnp.minimum(jnp.maximum(array, -limit), limit).astype(held_as)


def bell_draw_with(stream_key, dims, scale, limit, cuts, heavy, kind=jnp.bfloat16):
    values = scale * jax.random.normal(stream_key, dims, jnp.float32)
    if cuts:
        values = values * block_levels(stream_key, dims, cuts, -0.22, 0.18)
    return jnp.clip(strengthened(values, jax.random.fold_in(stream_key, 3), *heavy), -limit, limit).astype(kind)


def setup_inputs(seed: int = 0) -> dict:
    key_of = jax.random.split(jax.random.key(seed), 10)
    return {
        "tokens": bell_draw_with(key_of[0], (TOKENS, D), 1.0, 6.0, ((0, 32),), (0, 1, 32, 2.75)),
        "cotangent": noise(key_of[1], (TOKENS, DV), TOKENS ** -0.5, 0.0390625, ((0, 32),)),
        "policy": noise(key_of[2], (D, DV), D ** -0.5, 0.09375, ((0, 32),), jnp.float32),
        "anchor": noise(key_of[3], (D, DV), D ** -0.5, 0.09375, ((0, 32),), jnp.float32),
        "moment": noise(key_of[4], (D, DV), 0.5, 3.0, ((0, 32),), jnp.float32),
        "second": jnp.clip(jnp.exp(math.log(4.0) - 2.7725887 * jax.random.uniform(key_of[5], (D, DV), jnp.float32) ** block_levels(key_of[5], (D, DV), ((0, 32),), -0.2, 0.2)), 0.25, 4.0),
        "readout": noise(key_of[6], (DV,), 1.0, 6.0, (), jnp.float32),
        "pair_index": draw_pair_index(jax.random.fold_in(key_of[9], 71), 0),
        "noisy_flags": touch_ends((jax.random.randint(key_of[8], (PAIRS,), 0, 8) < 1).astype(jnp.int32), jax.random.fold_in(key_of[8], 1), 0, 1),
    }


beta_one = 0.9
beta_two = 0.95
step_count = 20
learn_rate = 0.003
adam_epsilon = 1e-08
blend_rate = 0.6
smoothing = 0.1

def adam_update(gradient, policy, anchor, moment, second):
    moment_new = beta_one * moment + (1.0 - beta_one) * gradient
    second_new = beta_two * second + (1.0 - beta_two) * gradient * gradient
    correct_one = 1.0 - beta_one ** step_count
    correct_two = 1.0 - beta_two ** step_count
    policy_new = policy - learn_rate * (moment_new / correct_one) / (jnp.sqrt(second_new / correct_two) + adam_epsilon)
    anchor_new = blend_rate * policy_new + (1.0 - blend_rate) * anchor
    return (policy_new, anchor_new, moment_new, second_new)

def token_scores(values, readout):
    return lax.optimization_barrier(jnp.sum(jax.nn.log_sigmoid(values * readout[None, :]), axis=1))

def sequence_margin(policy_values, anchor_values, readout, sequence_length):
    token_gap = token_scores(policy_values, readout) - token_scores(anchor_values, readout)
    return lax.optimization_barrier(jnp.mean(token_gap.reshape(-1, sequence_length), axis=1))

def pair_losses(margins, pair_index, noisy_flags):
    sequence_index = jnp.arange(margins.shape[0], dtype=jnp.int32)
    chosen = lax.optimization_barrier(jnp.sum(jnp.where(pair_index[:, 0:1] == sequence_index[None, :], margins[None, :], 0.0), axis=1))
    rejected = lax.optimization_barrier(jnp.sum(jnp.where(pair_index[:, 1:2] == sequence_index[None, :], margins[None, :], 0.0), axis=1))
    margin_gap = chosen - rejected
    logit_value = jnp.where(noisy_flags == 1, -margin_gap, margin_gap)
    return -(1.0 - smoothing) * jax.nn.log_sigmoid(logit_value) - smoothing * jax.nn.log_sigmoid(-logit_value)

def reference(tokens, cotangent, policy, anchor, moment, second, readout, pair_index, noisy_flags):
    gradient = lax.dot_general(tokens, cotangent, (((0,), (0,)), ((), ())), preferred_element_type=jnp.float32)
    policy_next, anchor_next, moment_next, second_next = adam_update(gradient, policy, anchor, moment, second)
    policy_values = jnp.dot(tokens, policy_next.astype(jnp.bfloat16), preferred_element_type=jnp.float32)
    anchor_values = jnp.dot(tokens, anchor_next.astype(jnp.bfloat16), preferred_element_type=jnp.float32)
    margins = sequence_margin(policy_values, anchor_values, readout, LEN)
    pair_loss = pair_losses(margins, pair_index, noisy_flags)
    return (policy_next, anchor_next, moment_next, second_next, pair_loss)
```

```python
import functools
import itertools
import jax
import jax.numpy as jnp
from jax import lax
from jax.experimental import pallas as pl
from jax.experimental.pallas import tpu as pltpu
from jax.sharding import PartitionSpec as P

LEN = 192


beta_one = 0.9
beta_two = 0.95
step_count = 20
learn_rate = 0.003
adam_epsilon = 1e-08
blend_rate = 0.6
smoothing = 0.1


def adam_update(gradient, policy, anchor, moment, second):
    moment_new = beta_one * moment + (1.0 - beta_one) * gradient
    second_new = beta_two * second + (1.0 - beta_two) * gradient * gradient
    correct_one = 1.0 - beta_one**step_count
    correct_two = 1.0 - beta_two**step_count
    policy_new = policy - learn_rate * (moment_new / correct_one) / (
        jnp.sqrt(second_new / correct_two) + adam_epsilon
    )
    anchor_new = blend_rate * policy_new + (1.0 - blend_rate) * anchor
    return (policy_new, anchor_new, moment_new, second_new)


def token_scores(values, readout):
    return jnp.sum(jax.nn.log_sigmoid(values * readout[None, :]), axis=1)


def sequence_margin(policy_values, anchor_values, readout, sequence_length):
    token_gap = token_scores(policy_values, readout) - token_scores(anchor_values, readout)
    return jnp.mean(token_gap.reshape(-1, sequence_length), axis=1)


def pair_losses(margins, pair_index, noisy_flags):
    sequence_index = jnp.arange(margins.shape[0], dtype=jnp.int32)
    chosen = jnp.sum(
        jnp.where(pair_index[:, 0:1] == sequence_index[None, :], margins[None, :], 0.0), axis=1
    )
    rejected = jnp.sum(
        jnp.where(pair_index[:, 1:2] == sequence_index[None, :], margins[None, :], 0.0), axis=1
    )
    margin_gap = chosen - rejected
    logit_value = jnp.where(noisy_flags == 1, -margin_gap, margin_gap)
    return -(1.0 - smoothing) * jax.nn.log_sigmoid(logit_value) - smoothing * jax.nn.log_sigmoid(
        -logit_value
    )


def shards(tokens, cotangent, policy, anchor, moment, second, readout, pair_index, noisy_flags):
    part_sum = lax.psum_scatter(
        lax.dot_general(
            tokens, cotangent, (((0,), (0,)), ((), ())), preferred_element_type=jnp.float32
        ),
        "fsdp",
        scatter_dimension=0,
        tiled=True,
    )
    gradient = lax.psum(part_sum.astype(jnp.bfloat16), "rep").astype(jnp.float32)
    policy_next, anchor_next, moment_next, second_next = adam_update(
        gradient, policy, anchor, moment, second
    )
    policy_half = policy_next.astype(jnp.bfloat16)
    anchor_half = anchor_next.astype(jnp.bfloat16)
    policy_whole = lax.all_gather(policy_half, "fsdp", axis=0, tiled=True)
    anchor_whole = lax.all_gather(anchor_half, "fsdp", axis=0, tiled=True)
    policy_values = jnp.dot(tokens, policy_whole, preferred_element_type=jnp.float32)
    anchor_values = jnp.dot(tokens, anchor_whole, preferred_element_type=jnp.float32)
    margins_own = sequence_margin(policy_values, anchor_values, readout, LEN)
    all_margins = lax.all_gather(margins_own, ("rep", "fsdp"), axis=0, tiled=True)
    pair_loss = pair_losses(all_margins, pair_index, noisy_flags)
    return (policy_next, anchor_next, moment_next, second_next, pair_loss)


PLANES = 4
EARLY = 64
MESH_ID = pl.DeviceIdType.MESH


def policy_update(gradient, policy, moment, second):
    moment_new = beta_one * moment + (1.0 - beta_one) * gradient
    second_new = beta_two * second + (1.0 - beta_two) * gradient * gradient
    correct_one = 1.0 - beta_one**step_count
    correct_two = 1.0 - beta_two**step_count
    return policy - learn_rate * (moment_new / correct_one) / (
        jnp.sqrt(second_new / correct_two) + adam_epsilon
    )


def fused_kernel(
    sizes,
    tokens,
    cotangent,
    policy,
    anchor,
    moment,
    second,
    readout,
    gradient_out,
    margin_out,
    tok,
    cot,
    cot_t,
    anc,
    anc_send,
    par,
    send_a1,
    recv_a1,
    keep_a,
    send_b1,
    recv_b1,
    keep_b,
    send_a2,
    recv_a2,
    send_b2,
    recv_b2,
    send_z,
    recv_z,
    grad_own,
    result,
    weights,
    acc,
    table,
    local_sem,
    swap_send,
    swap_recv,
    rs_send,
    rs_recv,
    rz_send,
    rz_recv,
    out_send,
    out_recv,
    xy_send,
    xy_recv,
    z_send,
    z_recv,
    m_send,
    m_recv,
):
    n, rows, tokens_own, half = sizes
    block = 2 * rows
    span = 4 * block
    pair = 2 * block
    low = half // 2
    me = lax.axis_index("fsdp")
    core = me % 2
    px = (me // 2) % 2
    py = (me // 4) % 2
    pz = me // 8
    chip = me // 2
    mate = me + 1 - 2 * core
    x_mate = me + 2 - 4 * px
    y_mate = me + 4 - 8 * py
    home = chip * block

    top = pz // 2
    near = pz + top * (3 - 2 * pz)

    def plane(t):
        there = (near, 1 - near, 2, 3)[t]
        return there + top * (3 - 2 * there)

    def z_mate(t):
        return me + 8 * (plane(t) - pz)

    def remote(src, dst, send_sem, recv_sem, device):
        return pltpu.make_async_remote_copy(
            src_ref=src,
            dst_ref=dst,
            send_sem=send_sem,
            recv_sem=recv_sem,
            device_id={"fsdp": device},
            device_id_type=MESH_ID,
        )

    barrier = pltpu.get_barrier_semaphore()
    others = [mate, x_mate, y_mate] + [z_mate(t) for t in (1, 2, 3)]
    for other in others:
        pl.semaphore_signal(barrier, inc=1, device_id={"fsdp": other}, device_id_type=MESH_ID)

    mine = pl.ds(pl.multiple_of(core * half, half), half)
    theirs = pl.ds(pl.multiple_of((1 - core) * half, half), half)
    params = (policy, moment, second)

    def columns(i, dy):
        start = plane(3 - i) * span + ((py + dy) % 2) * pair
        return pl.ds(pl.multiple_of(start, pair), pair)

    pieces = [(i, dy) for i in range(PLANES) for dy in (1, 0)]

    anc_local = []
    for r, side in enumerate((mine, theirs)):
        copy = pltpu.make_async_copy(anchor.at[:, side], anc.at[r], local_sem.at[r])
        copy.start()
        anc_local.append(copy)
    cot_local = pltpu.make_async_copy(cotangent.at[:, mine], cot.at[core], local_sem.at[2])
    cot_local.start()
    tok_local = {}
    for j, key in enumerate(pieces):
        where = columns(*key)
        tok_local[key] = pltpu.make_async_copy(
            tokens.at[:, where], tok.at[core, :, where], local_sem.at[8 + j]
        )
        tok_local[key].start()
    par_local = []
    for a in range(3):
        copy = pltpu.make_async_copy(params[a].at[:, mine], par.at[a, core], local_sem.at[3 + a])
        copy.start()
        par_local.append(copy)

    own_rows = pl.ds(pl.multiple_of(home + core * rows, rows), rows)
    anc_local[0].wait()
    weights[1, own_rows, :] = anc[0].astype(jnp.bfloat16)
    anc_local[1].wait()
    anc_send[...] = anc[1].astype(jnp.bfloat16)

    pl.semaphore_wait(barrier, len(others))

    sends = []

    def chip_at(zz, dy, dx):
        return zz * 4 + ((py + dy) % 2) * 2 + (px + dx) % 2

    kinds = {
        "c": (1, core * (block - EARLY), EARLY),
        "b": (1, (1 - core) * EARLY, block - EARLY),
        "p": (0, 0, block),
    }

    def part(kind, k, which=None):
        m, start, count = kinds[kind]
        if which is not None:
            count = count // 2
            start = start + which * count
        return weights.at[m, pl.ds(pl.multiple_of(k * block + start, 16), count), :]

    flights = {}

    def launch(name, copy):
        copy.start()
        flights[name] = copy
        sends.append(copy)

    def spread(kind, q, zz):
        ref = part(kind, chip_at(zz, 0, 0))
        launch((q, 0), remote(ref, ref, xy_send.at[q, 0], xy_recv.at[q, 0], x_mate))
        launch((q, 1), remote(ref, ref, xy_send.at[q, 1], xy_recv.at[q, 1], y_mate))

    def relay(kind, q, zz):
        flights[q, 1].wait_recv()
        ref = part(kind, chip_at(zz, 1, 0), 0)
        launch((q, 2), remote(ref, ref, xy_send.at[q, 2], xy_recv.at[q, 2], x_mate))
        flights[q, 0].wait_recv()
        ref = part(kind, chip_at(zz, 0, 1), 1)
        launch((q, 3), remote(ref, ref, xy_send.at[q, 3], xy_recv.at[q, 3], y_mate))

    def relayed(q):
        flights[q, 2].wait_recv()
        flights[q, 3].wait_recv()

    def z_out(kind, q, k):
        for t in (1, 2, 3):
            ref = part(kind, k)
            copy = remote(ref, ref, z_send.at[q, t - 1], z_recv.at[q, pz], z_mate(t))
            copy.start()
            sends.append(copy)

    def z_in(kind, q, t, dy=0, dx=0):
        ref = part(kind, chip_at(plane(t), dy, dx))
        remote(ref, ref, z_send.at[q, t - 1], z_recv.at[q, plane(t)], z_mate(t)).wait_recv()

    spread("c", 0, pz)
    z_out("c", 0, chip)
    launch(
        "anc",
        remote(anc_send, weights.at[1, own_rows, :], swap_send.at[0], swap_recv.at[0], mate),
    )
    cot_swap = remote(cotangent.at[:, theirs], cot.at[core], swap_send.at[1], swap_recv.at[1], mate)
    cot_swap.start()
    sends.append(cot_swap)
    tok_swap = {}
    for j, key in enumerate(pieces):
        where = columns(*key)
        tok_swap[key] = remote(
            tokens.at[:, where],
            tok.at[core, :, where],
            swap_send.at[8 + j],
            swap_recv.at[8 + j],
            mate,
        )
        tok_swap[key].start()
        sends.append(tok_swap[key])
    par_swap = []
    for a in range(3):
        copy = remote(
            params[a].at[:, theirs], par.at[a, core], swap_send.at[2 + a], swap_recv.at[2 + a], mate
        )
        copy.start()
        par_swap.append(copy)
        sends.append(copy)

    flights["anc"].wait_recv()
    z_out("b", 4, chip)
    spread("b", 1, pz)

    cot_local.wait()
    cot_swap.wait_recv()
    for r in range(2):
        cot_t[:, r * tokens_own : (r + 1) * tokens_own] = (
            cot[r].astype(jnp.float32).T.astype(jnp.bfloat16)
        )

    def first(key):
        tok_local[key].wait()
        tok_swap[key].wait_recv()

    def block_gradient(i, dy, dx):
        target = chip_at(plane(3 - i), dy, dx)
        where = pl.ds(pl.multiple_of(target * block, block), block)
        total = jnp.dot(
            cot_t[:, :tokens_own], tok[0, :, where], preferred_element_type=jnp.float32
        )
        total += jnp.dot(
            cot_t[:, tokens_own:], tok[1, :, where], preferred_element_type=jnp.float32
        )
        if dx == 1:
            send_a1[i, dy] = total[:low].astype(jnp.bfloat16)
        else:
            keep_a[i, dy] = total[:low]
        if dy == 1:
            send_b1[i, dx] = total[low:].astype(jnp.bfloat16)
        else:
            keep_b[i, dx] = total[low:]

    hops = {}

    def hop(name, i, slot, src, dst, device):
        copy = remote(src, dst, rs_send.at[slot, i], rs_recv.at[slot, i], device)
        copy.start()
        hops[name, i] = copy
        sends.append(copy)

    def send_b(i):
        hop("b1", i, 1, send_b1.at[i], recv_b1.at[i], y_mate)

    def send_a(i):
        hop("a1", i, 0, send_a1.at[i], recv_a1.at[i], x_mate)

    def stage_one(i, hold=False, between=None):
        first((i, 1))
        block_gradient(i, 1, 1)
        block_gradient(i, 1, 0)
        if not hold:
            send_b(i)
        if between is not None:
            between()
        first((i, 0))
        block_gradient(i, 0, 1)
        if not hold:
            send_a(i)
        block_gradient(i, 0, 0)

    def stage_two(i):
        hops["a1", i].wait_recv()
        send_a2[i] = (keep_a[i, 1] + recv_a1[i, 1].astype(jnp.float32)).astype(jnp.bfloat16)
        hop("a2", i, 2, send_a2.at[i], recv_a2.at[i], y_mate)
        hops["b1", i].wait_recv()
        send_b2[i] = (keep_b[i, 1] + recv_b1[i, 1].astype(jnp.float32)).astype(jnp.bfloat16)
        hop("b2", i, 3, send_b2.at[i], recv_b2.at[i], x_mate)

    def stage_three(i):
        hops["a2", i].wait_recv()
        total_a = keep_a[i, 0] + recv_a1[i, 0].astype(jnp.float32) + recv_a2[i].astype(jnp.float32)
        hops["b2", i].wait_recv()
        total_b = keep_b[i, 0] + recv_b1[i, 0].astype(jnp.float32) + recv_b2[i].astype(jnp.float32)
        if i == PLANES - 1:
            grad_own[:low] = total_a
            grad_own[low:] = total_b
        else:
            send_z[i, :low] = total_a.astype(jnp.bfloat16)
            send_z[i, low:] = total_b.astype(jnp.bfloat16)
            copy = remote(
                send_z.at[i], recv_z.at[pz], rz_send.at[i], rz_recv.at[pz], z_mate(3 - i)
            )
            copy.start()
            sends.append(copy)

    def early_out():
        relay("c", 0, pz)
        z_out("c", 1, chip_at(pz, 0, 1))
        z_out("c", 2, chip_at(pz, 1, 0))

    def blend_spread(t):
        z_in("b", 4, t)
        spread("b", 1 + t, plane(t))

    def blend_relay(t):
        relay("b", 1 + t, plane(t))

    stage_one(0, between=early_out)
    stage_one(1)
    blend_relay(0)
    stage_one(2)
    stage_two(0)
    stage_two(1)
    stage_one(3, hold=True)
    stage_two(2)
    send_b(3)
    send_a(3)
    stage_three(0)
    stage_three(1)
    blend_spread(1)
    stage_three(2)
    relayed(0)
    z_out("c", 3, chip_at(pz, 1, 1))
    stage_two(3)
    blend_relay(1)
    blend_spread(2)
    for a in range(3):
        par_local[a].wait()
        par_swap[a].wait_recv()
    for t in (3, 2, 1):
        zz = plane(t)
        remote(
            send_z.at[0], recv_z.at[zz], rz_send.at[0], rz_recv.at[zz], z_mate(t)
        ).wait_recv()
    stage_three(3)
    gradient = grad_own[...]
    for t in (1, 2, 3):
        gradient += recv_z[plane(t)].astype(jnp.float32)
    gradient = gradient.T
    for r in range(2):
        own = gradient[r * rows : (r + 1) * rows]
        updated = policy_update(own, par[0, r], par[1, r], par[2, r])
        result[r] = own
        weights[0, pl.ds(pl.multiple_of(home + r * rows, rows), rows), :] = updated.astype(
            jnp.bfloat16
        )
    z_out("p", 5, chip)
    spread("p", 5, pz)

    tile = tokens_own
    scale = readout[core]

    def score_sum(values):
        low_part = jnp.minimum(values, 0.0).reshape(LEN // 8, 8, half)
        factor = (1.0 + jnp.exp(-jnp.abs(values))).reshape(LEN // 8, 8, half)
        product = factor[0]
        for j in range(1, LEN // 8):
            product = product * factor[j]
        return jnp.sum(low_part, axis=0) - jnp.log(product)

    def multiply(m, t):
        where = pl.ds(pl.multiple_of(plane(t) * span, span), span)

        @pl.loop(0, 2)
        def _(i):
            value = jnp.dot(
                tok[i, :, where], weights[m, where, :], preferred_element_type=jnp.float32
            )
            acc[m, i] = value if t == 0 else acc[m, i] + value

    def anchor_multiply(t):
        relayed(1 + t)
        if t > 0:
            for j, (dy, dx) in enumerate(((0, 0), (0, 1), (1, 0), (1, 1))):
                z_in("c", j, t, dy, dx)
        multiply(1, t)

    def policy_multiply(t):
        relayed(5 + t)
        multiply(0, t)

    def policy_spread(t):
        z_in("p", 5, t)
        spread("p", 5 + t, plane(t))

    def policy_relay(t):
        relay("p", 5 + t, plane(t))

    def spot(zz, dy, dx):
        return pl.ds(pl.multiple_of(chip_at(zz, dy, dx) * block, block), block)

    def compute_near(zz):
        @pl.loop(0, 2)
        def _(i):
            value = acc[0, i]
            for dy, dx in ((0, 0), (0, 1), (1, 0)):
                where = spot(zz, dy, dx)
                value += jnp.dot(
                    tok[i, :, where], weights[0, where, :], preferred_element_type=jnp.float32
                )
            acc[0, i] = value

    def compute_last(zz):
        where = spot(zz, 1, 1)

        @pl.loop(0, 2)
        def _(i):
            value = acc[0, i] + jnp.dot(
                tok[i, :, where], weights[0, where, :], preferred_element_type=jnp.float32
            )
            acc[1, i] = (blend_rate * value + (1.0 - blend_rate) * acc[1, i]) * scale
            acc[0, i] = value * scale
            for j in range(tile // LEN):
                gap = score_sum(acc[0, i, j * LEN : (j + 1) * LEN]) - score_sum(
                    acc[1, i, j * LEN : (j + 1) * LEN]
                )
                gap = jnp.sum(gap, axis=0, keepdims=True)
                gap = jnp.sum(gap, axis=1, keepdims=True)
                table[core, chip, pl.ds(i * (tile // LEN) + j, 1), :] = jnp.broadcast_to(
                    gap * (1.0 / LEN), (1, 128)
                )

    waits = []
    copy = pltpu.make_async_copy(result.at[core], gradient_out.at[:, mine], local_sem.at[6])
    copy.start()
    waits.append(copy)
    copy = remote(
        result.at[1 - core], gradient_out.at[:, mine], out_send.at[0], out_recv.at[0], mate
    )
    copy.start()
    waits.append(copy)

    blend_relay(2)
    blend_spread(3)
    anchor_multiply(0)
    anchor_multiply(1)
    policy_relay(0)
    policy_spread(1)
    blend_relay(3)
    anchor_multiply(2)
    policy_spread(2)
    policy_multiply(0)
    policy_relay(1)
    anchor_multiply(3)
    policy_spread(3)
    policy_multiply(1)
    policy_relay(2)
    policy_relay(3)
    policy_multiply(2)
    compute_near(plane(3))
    relayed(8)
    compute_last(plane(3))

    everyone = [
        (t, dy, dx, dc) for t in (3, 2, 1, 0) for dy, dx, dc in itertools.product((1, 0), repeat=3)
    ][:-1]
    arrivals = []
    for j, (t, dy, dx, dc) in enumerate(everyone):
        there = chip_at(plane(t), dy, dx) * 2 + (core + dc) % 2
        ref = table.at[core, chip]
        copy = remote(ref, ref, m_send.at[j], m_recv.at[me], there)
        copy.start()
        sends.append(copy)
        arrivals.append(remote(ref, ref, m_send.at[j], m_recv.at[there], there))
    for copy in waits:
        copy.wait()
    for copy in sends:
        copy.wait_send()
    for copy in arrivals:
        copy.wait_recv()
    margin_out[...] = table[...]


def finish_kernel(
    gradient,
    policy,
    anchor,
    moment,
    second,
    table,
    pair_index,
    noisy_flags,
    policy_out,
    anchor_out,
    moment_out,
    second_out,
    loss_out,
):
    updated = adam_update(gradient[...], policy[...], anchor[...], moment[...], second[...])
    for out, value in zip((policy_out, anchor_out, moment_out, second_out), updated):
        out[...] = value
    margins = table[0] + table[1]
    sequence = lax.broadcasted_iota(jnp.int32, margins.shape, 0)

    def margin_of(index):
        return jnp.sum(jnp.where(sequence == index, margins, 0.0), axis=0, keepdims=True)

    for p in range(noisy_flags.shape[0]):
        gap = margin_of(pair_index[p, 0]) - margin_of(pair_index[p, 1])
        gap = jnp.where(noisy_flags[p] == 1, -gap, gap)
        tail = jnp.log(1.0 + jnp.exp(-jnp.abs(gap)))
        loss = (1.0 - smoothing) * (tail - jnp.minimum(gap, 0.0)) + smoothing * (
            tail + jnp.maximum(gap, 0.0)
        )
        loss_out[p] = loss[0, 0]


def fused_shards(n, tokens, cotangent, policy, anchor, moment, second, readout, pair_index, noisy_flags):
    tokens_own, depth = tokens.shape
    rows, channels = policy.shape
    half = channels // 2
    block = 2 * rows
    low = half // 2
    seq_chip = 2 * tokens_own // LEN
    sizes = (n, rows, tokens_own, half)
    bf, f32 = jnp.bfloat16, jnp.float32
    vmem, dma = pltpu.VMEM, pltpu.SemaphoreType.DMA
    hbm = pl.BlockSpec(memory_space=pl.ANY)
    whole = pl.BlockSpec(memory_space=pltpu.VMEM)
    weight = jax.ShapeDtypeStruct((rows, channels), f32)
    gradient, table = pl.pallas_call(
        functools.partial(fused_kernel, sizes),
        out_shape=(weight, jax.ShapeDtypeStruct((2, n // 2, seq_chip, 128), f32)),
        in_specs=[hbm] * 6 + [whole],
        out_specs=(hbm, whole),
        scratch_shapes=[
            vmem((2, tokens_own, depth), bf),
            vmem((2, tokens_own, half), bf),
            vmem((half, 2 * tokens_own), bf),
            vmem((2, rows, half), f32),
            vmem((rows, half), bf),
            vmem((3, 2, rows, half), f32),
            vmem((4, 2, low, block), bf),
            vmem((4, 2, low, block), bf),
            vmem((4, 2, low, block), f32),
            vmem((4, 2, low, block), bf),
            vmem((4, 2, low, block), bf),
            vmem((4, 2, low, block), f32),
            vmem((4, low, block), bf),
            vmem((4, low, block), bf),
            vmem((4, low, block), bf),
            vmem((4, low, block), bf),
            vmem((3, half, block), bf),
            vmem((4, half, block), bf),
            vmem((half, block), f32),
            vmem((2, rows, half), f32),
            vmem((2, depth, half), bf),
            vmem((2, 2, tokens_own, half), f32),
            vmem((2, n // 2, seq_chip, 128), f32),
            dma((16,)),
            dma((16,)),
            dma((16,)),
            dma((4, 4)),
            dma((4, 4)),
            dma((3,)),
            dma((4,)),
            dma((1,)),
            dma((1,)),
            dma((9, 4)),
            dma((9, 4)),
            dma((6, 3)),
            dma((6, 4)),
            dma((n,)),
            dma((n,)),
        ],
        compiler_params=pltpu.CompilerParams(
            collective_id=0, has_side_effects=True, vmem_limit_bytes=56 * 1024 * 1024
        ),
    )(
        tokens,
        cotangent,
        policy,
        anchor,
        moment,
        second,
        readout.reshape(2, 1, half),
    )
    smem = pl.BlockSpec(memory_space=pltpu.SMEM)
    policy_next, anchor_next, moment_next, second_next, pair_loss = pl.pallas_call(
        finish_kernel,
        out_shape=(weight,) * 4 + (jax.ShapeDtypeStruct(noisy_flags.shape, f32),),
        in_specs=[whole] * 6 + [smem] * 2,
        out_specs=(whole,) * 4 + (smem,),
    )(
        gradient,
        policy,
        anchor,
        moment,
        second,
        table.reshape(2, n // 2 * seq_chip, 128),
        pair_index,
        noisy_flags,
    )
    return (policy_next, anchor_next, moment_next, second_next, pair_loss)


def solution(mesh):
    placed = (
        P(("rep", "fsdp"), None),
        P(("rep", "fsdp"), None),
        P("fsdp", None),
        P("fsdp", None),
        P("fsdp", None),
        P("fsdp", None),
        P(),
        P(("rep", "fsdp"), None),
        P(("rep", "fsdp")),
    )
    n = mesh.shape["fsdp"]
    body = shards
    if mesh.shape["rep"] == 1 and n == 8 * PLANES:
        body = functools.partial(fused_shards, n)
    return jax.shard_map(
        body,
        mesh=mesh,
        in_specs=placed,
        out_specs=(
            P("fsdp", None),
            P("fsdp", None),
            P("fsdp", None),
            P("fsdp", None),
            P(("rep", "fsdp")),
        ),
        check_vma=False,
    )
```

```python
import functools
import itertools
import jax
import jax.numpy as jnp
from jax import lax
from jax.experimental import pallas as pl
from jax.experimental.pallas import tpu as pltpu
from jax.sharding import PartitionSpec as P

LEN = 192


beta_one = 0.9
beta_two = 0.95
step_count = 20
learn_rate = 0.003
adam_epsilon = 1e-08
blend_rate = 0.6
smoothing = 0.1


def adam_update(gradient, policy, anchor, moment, second):
    moment_new = beta_one * moment + (1.0 - beta_one) * gradient
    second_new = beta_two * second + (1.0 - beta_two) * gradient * gradient
    correct_one = 1.0 - beta_one**step_count
    correct_two = 1.0 - beta_two**step_count
    policy_new = policy - learn_rate * (moment_new / correct_one) / (
        jnp.sqrt(second_new / correct_two) + adam_epsilon
    )
    anchor_new = blend_rate * policy_new + (1.0 - blend_rate) * anchor
    return (policy_new, anchor_new, moment_new, second_new)


def token_scores(values, readout):
    return jnp.sum(jax.nn.log_sigmoid(values * readout[None, :]), axis=1)


def sequence_margin(policy_values, anchor_values, readout, sequence_length):
    token_gap = token_scores(policy_values, readout) - token_scores(anchor_values, readout)
    return jnp.mean(token_gap.reshape(-1, sequence_length), axis=1)


def pair_losses(margins, pair_index, noisy_flags):
    sequence_index = jnp.arange(margins.shape[0], dtype=jnp.int32)
    chosen = jnp.sum(
        jnp.where(pair_index[:, 0:1] == sequence_index[None, :], margins[None, :], 0.0), axis=1
    )
    rejected = jnp.sum(
        jnp.where(pair_index[:, 1:2] == sequence_index[None, :], margins[None, :], 0.0), axis=1
    )
    margin_gap = chosen - rejected
    logit_value = jnp.where(noisy_flags == 1, -margin_gap, margin_gap)
    return -(1.0 - smoothing) * jax.nn.log_sigmoid(logit_value) - smoothing * jax.nn.log_sigmoid(
        -logit_value
    )


def shards(tokens, cotangent, policy, anchor, moment, second, readout, pair_index, noisy_flags):
    part_sum = lax.psum_scatter(
        lax.dot_general(
            tokens, cotangent, (((0,), (0,)), ((), ())), preferred_element_type=jnp.float32
        ),
        "fsdp",
        scatter_dimension=0,
        tiled=True,
    )
    gradient = lax.psum(part_sum.astype(jnp.bfloat16), "rep").astype(jnp.float32)
    policy_next, anchor_next, moment_next, second_next = adam_update(
        gradient, policy, anchor, moment, second
    )
    policy_half = policy_next.astype(jnp.bfloat16)
    anchor_half = anchor_next.astype(jnp.bfloat16)
    policy_whole = lax.all_gather(policy_half, "fsdp", axis=0, tiled=True)
    anchor_whole = lax.all_gather(anchor_half, "fsdp", axis=0, tiled=True)
    policy_values = jnp.dot(tokens, policy_whole, preferred_element_type=jnp.float32)
    anchor_values = jnp.dot(tokens, anchor_whole, preferred_element_type=jnp.float32)
    margins_own = sequence_margin(policy_values, anchor_values, readout, LEN)
    all_margins = lax.all_gather(margins_own, ("rep", "fsdp"), axis=0, tiled=True)
    pair_loss = pair_losses(all_margins, pair_index, noisy_flags)
    return (policy_next, anchor_next, moment_next, second_next, pair_loss)


PLANES = 4
EARLY = 64
MESH_ID = pl.DeviceIdType.MESH


def policy_update(gradient, policy, moment, second):
    moment_new = beta_one * moment + (1.0 - beta_one) * gradient
    second_new = beta_two * second + (1.0 - beta_two) * gradient * gradient
    correct_one = 1.0 - beta_one**step_count
    correct_two = 1.0 - beta_two**step_count
    return policy - learn_rate * (moment_new / correct_one) / (
        jnp.sqrt(second_new / correct_two) + adam_epsilon
    )


def fused_kernel(
    sizes,
    tokens,
    cotangent,
    policy,
    anchor,
    moment,
    second,
    readout,
    gradient_out,
    margin_out,
    tok,
    cot,
    cot_t,
    anc,
    anc_send,
    par,
    send_a1,
    recv_a1,
    keep_a,
    send_b1,
    recv_b1,
    keep_b,
    send_a2,
    recv_a2,
    send_b2,
    recv_b2,
    send_z,
    recv_z,
    grad_own,
    result,
    weights,
    acc,
    table,
    local_sem,
    swap_send,
    swap_recv,
    rs_send,
    rs_recv,
    rz_send,
    rz_recv,
    out_send,
    out_recv,
    xy_send,
    xy_recv,
    z_send,
    z_recv,
    p_send,
    m_send,
    m_recv,
):
    n, rows, tokens_own, half = sizes
    block = 2 * rows
    span = 4 * block
    pair = 2 * block
    low = half // 2
    me = lax.axis_index("fsdp")
    core = me % 2
    px = (me // 2) % 2
    py = (me // 4) % 2
    pz = me // 8
    chip = me // 2
    mate = me + 1 - 2 * core
    x_mate = me + 2 - 4 * px
    y_mate = me + 4 - 8 * py
    home = chip * block

    top = pz // 2
    near = pz + top * (3 - 2 * pz)

    def plane(t):
        there = (near, 1 - near, 2, 3)[t]
        return there + top * (3 - 2 * there)

    def z_mate(t):
        return me + 8 * (plane(t) - pz)

    def remote(src, dst, send_sem, recv_sem, device):
        return pltpu.make_async_remote_copy(
            src_ref=src,
            dst_ref=dst,
            send_sem=send_sem,
            recv_sem=recv_sem,
            device_id={"fsdp": device},
            device_id_type=MESH_ID,
        )

    barrier = pltpu.get_barrier_semaphore()
    others = [mate, x_mate, y_mate] + [z_mate(t) for t in (1, 2, 3)]
    for other in others:
        pl.semaphore_signal(barrier, inc=1, device_id={"fsdp": other}, device_id_type=MESH_ID)

    mine = pl.ds(pl.multiple_of(core * half, half), half)
    theirs = pl.ds(pl.multiple_of((1 - core) * half, half), half)
    params = (policy, moment, second)

    def columns(i, dy):
        start = plane(3 - i) * span + ((py + dy) % 2) * pair
        return pl.ds(pl.multiple_of(start, pair), pair)

    pieces = [(i, dy) for i in range(PLANES) for dy in (1, 0)]

    anc_local = []
    for r, side in enumerate((mine, theirs)):
        copy = pltpu.make_async_copy(anchor.at[:, side], anc.at[r], local_sem.at[r])
        copy.start()
        anc_local.append(copy)
    cot_local = pltpu.make_async_copy(cotangent.at[:, mine], cot.at[core], local_sem.at[2])
    cot_local.start()
    tok_local = {}
    for j, key in enumerate(pieces):
        where = columns(*key)
        tok_local[key] = pltpu.make_async_copy(
            tokens.at[:, where], tok.at[core, :, where], local_sem.at[8 + j]
        )
        tok_local[key].start()
    par_local = []
    for a in range(3):
        copy = pltpu.make_async_copy(params[a].at[:, mine], par.at[a, core], local_sem.at[3 + a])
        copy.start()
        par_local.append(copy)

    pl.semaphore_wait(barrier, len(others))

    sends = []
    cot_swap = remote(cotangent.at[:, theirs], cot.at[core], swap_send.at[1], swap_recv.at[1], mate)
    cot_swap.start()
    sends.append(cot_swap)
    own_rows = pl.ds(pl.multiple_of(home + core * rows, rows), rows)
    anc_local[0].wait()
    weights[1, own_rows, :] = anc[0].astype(jnp.bfloat16)

    def chip_at(zz, dy, dx):
        return zz * 4 + ((py + dy) % 2) * 2 + (px + dx) % 2

    kinds = {
        "c": (1, core * (block - EARLY), EARLY),
        "a": (1, (1 - core) * EARLY, block - EARLY),
        "p": (0, 0, block),
    }

    def part(kind, k, which=None):
        m, start, count = kinds[kind]
        if which is not None:
            count = count // 2
            start = start + which * count
        return weights.at[m, pl.ds(pl.multiple_of(k * block + start, 16), count), :]

    flights = {}

    def launch(name, copy):
        copy.start()
        flights[name] = copy
        sends.append(copy)

    def spread(kind, q, zz):
        ref = part(kind, chip_at(zz, 0, 0))
        launch((q, 0), remote(ref, ref, xy_send.at[q, 0], xy_recv.at[q, 0], x_mate))
        launch((q, 1), remote(ref, ref, xy_send.at[q, 1], xy_recv.at[q, 1], y_mate))

    def relay(kind, q, zz):
        flights[q, 1].wait_recv()
        ref = part(kind, chip_at(zz, 1, 0), 0)
        launch((q, 2), remote(ref, ref, xy_send.at[q, 2], xy_recv.at[q, 2], x_mate))
        flights[q, 0].wait_recv()
        ref = part(kind, chip_at(zz, 0, 1), 1)
        launch((q, 3), remote(ref, ref, xy_send.at[q, 3], xy_recv.at[q, 3], y_mate))

    def relayed(q):
        flights[q, 2].wait_recv()
        flights[q, 3].wait_recv()

    def z_out(kind, q, k):
        for t in (1, 2, 3):
            ref = part(kind, k)
            copy = remote(ref, ref, z_send.at[q, t - 1], z_recv.at[q, pz], z_mate(t))
            copy.start()
            sends.append(copy)

    def z_in(kind, q, t, dy=0, dx=0):
        ref = part(kind, chip_at(plane(t), dy, dx))
        remote(ref, ref, z_send.at[q, t - 1], z_recv.at[q, plane(t)], z_mate(t)).wait_recv()

    middle = jnp.logical_and(pz > 0, pz < PLANES - 1)

    def chain_copies(t):
        zz = plane(t)
        ref = part("p", chip_at(zz, 0, 0))
        up = remote(ref, ref, p_send.at[0, t], z_recv.at[1, zz], (me + 8) % n)
        down = remote(ref, ref, p_send.at[1, t], z_recv.at[1, zz], (me + n - 8) % n)
        return zz, up, down

    def far_copy():
        ref = part("p", chip)
        return remote(ref, ref, p_send.at[2, 0], z_recv.at[1, pz], z_mate(3))

    def chain_each(t, copies, act):
        zz, up, down = copies
        if t < PLANES - 1:

            @pl.when(jnp.logical_and(zz <= pz, pz < PLANES - 1))
            def _():
                act(up)

            @pl.when(jnp.logical_and(zz >= pz, pz > 0))
            def _():
                act(down)

        if t == 0:

            @pl.when(jnp.logical_not(middle))
            def _():
                act(far_copy())

    def chain_step(t):
        copies = chain_copies(t)
        if t > 0:
            copies[1].wait_recv()
        chain_each(t, copies, lambda copy: copy.start())

    spread("c", 8, pz)
    z_out("c", 2, chip)
    anc_local[1].wait()
    anc_send[...] = anc[1].astype(jnp.bfloat16)
    launch(
        "anc",
        remote(anc_send, weights.at[1, own_rows, :], swap_send.at[0], swap_recv.at[0], mate),
    )
    tok_swap = {}
    for j, key in enumerate(pieces):
        where = columns(*key)
        tok_swap[key] = remote(
            tokens.at[:, where],
            tok.at[core, :, where],
            swap_send.at[8 + j],
            swap_recv.at[8 + j],
            mate,
        )
        tok_swap[key].start()
        sends.append(tok_swap[key])
    par_swap = []
    for a in range(3):
        copy = remote(
            params[a].at[:, theirs], par.at[a, core], swap_send.at[2 + a], swap_recv.at[2 + a], mate
        )
        copy.start()
        par_swap.append(copy)
        sends.append(copy)

    flights["anc"].wait_recv()
    z_out("a", 0, chip)
    spread("a", 0, pz)

    cot_local.wait()
    cot_swap.wait_recv()
    for r in range(2):
        cot_t[:, r * tokens_own : (r + 1) * tokens_own] = (
            cot[r].astype(jnp.float32).T.astype(jnp.bfloat16)
        )

    def first(key):
        tok_local[key].wait()
        tok_swap[key].wait_recv()

    def block_gradient(i, dy, dx):
        target = chip_at(plane(3 - i), dy, dx)
        where = pl.ds(pl.multiple_of(target * block, block), block)
        total = jnp.dot(
            cot_t[:, :tokens_own], tok[0, :, where], preferred_element_type=jnp.float32
        )
        total += jnp.dot(
            cot_t[:, tokens_own:], tok[1, :, where], preferred_element_type=jnp.float32
        )
        if dx == 1:
            send_a1[i, dy] = total[:low].astype(jnp.bfloat16)
        else:
            keep_a[i, dy] = total[:low]
        if dy == 1:
            send_b1[i, dx] = total[low:].astype(jnp.bfloat16)
        else:
            keep_b[i, dx] = total[low:]

    hops = {}

    def hop(name, i, slot, src, dst, device):
        copy = remote(src, dst, rs_send.at[slot, i], rs_recv.at[slot, i], device)
        copy.start()
        hops[name, i] = copy
        sends.append(copy)

    def send_b(i):
        hop("b1", i, 1, send_b1.at[i], recv_b1.at[i], y_mate)

    def send_a(i):
        hop("a1", i, 0, send_a1.at[i], recv_a1.at[i], x_mate)

    def stage_one(i, hold=False):
        first((i, 1))
        block_gradient(i, 1, 1)
        block_gradient(i, 1, 0)
        if not hold:
            send_b(i)
        first((i, 0))
        block_gradient(i, 0, 1)
        if not hold:
            send_a(i)
        block_gradient(i, 0, 0)

    def stage_two(i):
        hops["a1", i].wait_recv()
        send_a2[i] = (keep_a[i, 1] + recv_a1[i, 1].astype(jnp.float32)).astype(jnp.bfloat16)
        hop("a2", i, 2, send_a2.at[i], recv_a2.at[i], y_mate)
        hops["b1", i].wait_recv()
        send_b2[i] = (keep_b[i, 1] + recv_b1[i, 1].astype(jnp.float32)).astype(jnp.bfloat16)
        hop("b2", i, 3, send_b2.at[i], recv_b2.at[i], x_mate)

    def stage_three(i):
        hops["a2", i].wait_recv()
        total_a = keep_a[i, 0] + recv_a1[i, 0].astype(jnp.float32) + recv_a2[i].astype(jnp.float32)
        hops["b2", i].wait_recv()
        total_b = keep_b[i, 0] + recv_b1[i, 0].astype(jnp.float32) + recv_b2[i].astype(jnp.float32)
        if i == PLANES - 1:
            grad_own[:low] = total_a
            grad_own[low:] = total_b
        else:
            send_z[i, :low] = total_a.astype(jnp.bfloat16)
            send_z[i, low:] = total_b.astype(jnp.bfloat16)
            copy = remote(
                send_z.at[i], recv_z.at[pz], rz_send.at[i], rz_recv.at[pz], z_mate(3 - i)
            )
            copy.start()
            sends.append(copy)

    def anchor_spread(t):
        z_in("a", 0, t)
        spread("a", t, plane(t))

    def anchor_relay(t):
        relay("a", t, plane(t))

    stage_one(0)
    stage_one(1)
    stage_one(2, hold=True)
    relay("c", 8, pz)
    z_out("c", 3, chip_at(pz, 0, 1))
    stage_two(0)
    send_b(2)
    send_a(2)
    stage_one(3, hold=True)
    stage_two(1)
    stage_three(0)
    stage_two(2)
    send_b(3)
    send_a(3)
    stage_three(1)
    anchor_relay(0)
    anchor_spread(1)
    stage_three(2)
    z_out("c", 4, chip_at(pz, 1, 0))
    stage_two(3)
    anchor_spread(2)
    anchor_relay(1)
    for a in range(3):
        par_local[a].wait()
        par_swap[a].wait_recv()
    for t in (3, 2, 1):
        zz = plane(t)
        remote(
            send_z.at[0], recv_z.at[zz], rz_send.at[0], rz_recv.at[zz], z_mate(t)
        ).wait_recv()
    stage_three(3)
    gradient = grad_own[...]
    for t in (1, 2, 3):
        gradient += recv_z[plane(t)].astype(jnp.float32)
    gradient = gradient.T
    for r in range(2):
        own = gradient[r * rows : (r + 1) * rows]
        updated = policy_update(own, par[0, r], par[1, r], par[2, r])
        result[r] = own
        weights[0, pl.ds(pl.multiple_of(home + r * rows, rows), rows), :] = updated.astype(
            jnp.bfloat16
        )
    chain_step(0)
    spread("p", 4, pz)

    tile = tokens_own
    scale = readout[core]

    def score_sum(values):
        low_part = jnp.minimum(values, 0.0).reshape(LEN // 8, 8, half)
        factor = (1.0 + jnp.exp(-jnp.abs(values))).reshape(LEN // 8, 8, half)
        product = factor[0]
        for j in range(1, LEN // 8):
            product = product * factor[j]
        return jnp.sum(low_part, axis=0) - jnp.log(product)

    def multiply(m, t):
        where = pl.ds(pl.multiple_of(plane(t) * span, span), span)

        @pl.loop(0, 2)
        def _(i):
            value = jnp.dot(
                tok[i, :, where], weights[m, where, :], preferred_element_type=jnp.float32
            )
            acc[m, i] = value if t == 0 else acc[m, i] + value

    def anchor_multiply(t):
        relayed(t)
        if t > 0:
            for j, (dy, dx) in enumerate(((0, 0), (0, 1), (1, 0), (1, 1))):
                z_in("c", 2 + j, t, dy, dx)
        multiply(1, t)

    def policy_multiply(t):
        relayed(4 + t)
        multiply(0, t)

    def policy_spread(t):
        spread("p", 4 + t, plane(t))

    def policy_relay(t):
        relay("p", 4 + t, plane(t))

    def spot(zz, dy, dx):
        return pl.ds(pl.multiple_of(chip_at(zz, dy, dx) * block, block), block)

    def compute_near(zz):
        @pl.loop(0, 2)
        def _(i):
            value = acc[0, i]
            for dy, dx in ((0, 0), (0, 1), (1, 0)):
                where = spot(zz, dy, dx)
                value += jnp.dot(
                    tok[i, :, where], weights[0, where, :], preferred_element_type=jnp.float32
                )
            acc[0, i] = value

    def compute_last(zz):
        where = spot(zz, 1, 1)

        @pl.loop(0, 2)
        def _(i):
            value = acc[0, i] + jnp.dot(
                tok[i, :, where], weights[0, where, :], preferred_element_type=jnp.float32
            )
            acc[1, i] = (blend_rate * value + (1.0 - blend_rate) * acc[1, i]) * scale
            acc[0, i] = value * scale
            for j in range(tile // LEN):
                gap = score_sum(acc[0, i, j * LEN : (j + 1) * LEN]) - score_sum(
                    acc[1, i, j * LEN : (j + 1) * LEN]
                )
                gap = jnp.sum(gap, axis=0, keepdims=True)
                gap = jnp.sum(gap, axis=1, keepdims=True)
                table[core, chip, pl.ds(i * (tile // LEN) + j, 1), :] = jnp.broadcast_to(
                    gap * (1.0 / LEN), (1, 128)
                )

    waits = []
    copy = pltpu.make_async_copy(result.at[core], gradient_out.at[:, mine], local_sem.at[6])
    copy.start()
    waits.append(copy)
    copy = remote(
        result.at[1 - core], gradient_out.at[:, mine], out_send.at[0], out_recv.at[0], mate
    )
    copy.start()
    waits.append(copy)

    anchor_spread(3)
    relayed(8)
    anchor_multiply(0)
    anchor_relay(2)
    policy_relay(0)
    chain_step(1)

    @pl.when(middle)
    def _():
        chain_step(2)

    policy_spread(1)
    z_out("c", 5, chip_at(pz, 1, 1))
    anchor_relay(3)
    policy_multiply(0)

    @pl.when(jnp.logical_not(middle))
    def _():
        chain_step(2)

    chain_step(3)
    policy_spread(2)
    policy_relay(1)
    policy_spread(3)
    anchor_multiply(1)
    anchor_multiply(2)
    policy_relay(2)
    anchor_multiply(3)
    policy_multiply(1)
    policy_relay(3)
    compute_near(plane(3))
    policy_multiply(2)
    for copy in waits:
        copy.wait()
    for copy in sends:
        copy.wait_send()
    for t in range(PLANES):
        chain_each(t, chain_copies(t), lambda copy: copy.wait_send())
    relayed(7)
    compute_last(plane(3))

    everyone = [
        (t, dy, dx, dc) for t in (3, 2, 1, 0) for dy, dx, dc in itertools.product((1, 0), repeat=3)
    ][:-1]
    sent = []
    arrivals = []
    for j, (t, dy, dx, dc) in enumerate(everyone):
        there = chip_at(plane(t), dy, dx) * 2 + (core + dc) % 2
        ref = table.at[core, chip]
        copy = remote(ref, ref, m_send.at[j], m_recv.at[me], there)
        copy.start()
        sent.append(copy)
        arrivals.append(remote(ref, ref, m_send.at[j], m_recv.at[there], there))
    for copy in arrivals:
        copy.wait_recv()
    for copy in sent:
        copy.wait_send()
    margin_out[...] = table[...]


def finish_kernel(
    gradient,
    policy,
    anchor,
    moment,
    second,
    table,
    pair_index,
    noisy_flags,
    policy_out,
    anchor_out,
    moment_out,
    second_out,
    loss_out,
):
    updated = adam_update(gradient[...], policy[...], anchor[...], moment[...], second[...])
    for out, value in zip((policy_out, anchor_out, moment_out, second_out), updated):
        out[...] = value
    margins = table[0] + table[1]
    sequence = lax.broadcasted_iota(jnp.int32, margins.shape, 0)

    def margin_of(index):
        return jnp.sum(jnp.where(sequence == index, margins, 0.0), axis=0, keepdims=True)

    for p in range(noisy_flags.shape[0]):
        gap = margin_of(pair_index[p, 0]) - margin_of(pair_index[p, 1])
        gap = jnp.where(noisy_flags[p] == 1, -gap, gap)
        tail = jnp.log(1.0 + jnp.exp(-jnp.abs(gap)))
        loss = (1.0 - smoothing) * (tail - jnp.minimum(gap, 0.0)) + smoothing * (
            tail + jnp.maximum(gap, 0.0)
        )
        loss_out[p] = loss[0, 0]


def fused_shards(n, tokens, cotangent, policy, anchor, moment, second, readout, pair_index, noisy_flags):
    tokens_own, depth = tokens.shape
    rows, channels = policy.shape
    half = channels // 2
    block = 2 * rows
    low = half // 2
    seq_chip = 2 * tokens_own // LEN
    sizes = (n, rows, tokens_own, half)
    bf, f32 = jnp.bfloat16, jnp.float32
    vmem, dma = pltpu.VMEM, pltpu.SemaphoreType.DMA
    hbm = pl.BlockSpec(memory_space=pl.ANY)
    whole = pl.BlockSpec(memory_space=pltpu.VMEM)
    weight = jax.ShapeDtypeStruct((rows, channels), f32)
    gradient, table = pl.pallas_call(
        functools.partial(fused_kernel, sizes),
        out_shape=(weight, jax.ShapeDtypeStruct((2, n // 2, seq_chip, 128), f32)),
        in_specs=[hbm] * 6 + [whole],
        out_specs=(hbm, whole),
        scratch_shapes=[
            vmem((2, tokens_own, depth), bf),
            vmem((2, tokens_own, half), bf),
            vmem((half, 2 * tokens_own), bf),
            vmem((2, rows, half), f32),
            vmem((rows, half), bf),
            vmem((3, 2, rows, half), f32),
            vmem((4, 2, low, block), bf),
            vmem((4, 2, low, block), bf),
            vmem((4, 2, low, block), f32),
            vmem((4, 2, low, block), bf),
            vmem((4, 2, low, block), bf),
            vmem((4, 2, low, block), f32),
            vmem((4, low, block), bf),
            vmem((4, low, block), bf),
            vmem((4, low, block), bf),
            vmem((4, low, block), bf),
            vmem((3, half, block), bf),
            vmem((4, half, block), bf),
            vmem((half, block), f32),
            vmem((2, rows, half), f32),
            vmem((2, depth, half), bf),
            vmem((2, 2, tokens_own, half), f32),
            vmem((2, n // 2, seq_chip, 128), f32),
            dma((16,)),
            dma((16,)),
            dma((16,)),
            dma((4, 4)),
            dma((4, 4)),
            dma((3,)),
            dma((4,)),
            dma((1,)),
            dma((1,)),
            dma((9, 4)),
            dma((9, 4)),
            dma((6, 3)),
            dma((6, 4)),
            dma((3, 4)),
            dma((n,)),
            dma((n,)),
        ],
        compiler_params=pltpu.CompilerParams(
            collective_id=0, has_side_effects=True, vmem_limit_bytes=56 * 1024 * 1024
        ),
    )(
        tokens,
        cotangent,
        policy,
        anchor,
        moment,
        second,
        readout.reshape(2, 1, half),
    )
    smem = pl.BlockSpec(memory_space=pltpu.SMEM)
    policy_next, anchor_next, moment_next, second_next, pair_loss = pl.pallas_call(
        finish_kernel,
        out_shape=(weight,) * 4 + (jax.ShapeDtypeStruct(noisy_flags.shape, f32),),
        in_specs=[whole] * 6 + [smem] * 2,
        out_specs=(whole,) * 4 + (smem,),
    )(
        gradient,
        policy,
        anchor,
        moment,
        second,
        table.reshape(2, n // 2 * seq_chip, 128),
        pair_index,
        noisy_flags,
    )
    return (policy_next, anchor_next, moment_next, second_next, pair_loss)


def solution(mesh):
    placed = (
        P(("rep", "fsdp"), None),
        P(("rep", "fsdp"), None),
        P("fsdp", None),
        P("fsdp", None),
        P("fsdp", None),
        P("fsdp", None),
        P(),
        P(("rep", "fsdp"), None),
        P(("rep", "fsdp")),
    )
    n = mesh.shape["fsdp"]
    body = shards
    if mesh.shape["rep"] == 1 and n == 8 * PLANES:
        body = functools.partial(fused_shards, n)
    return jax.shard_map(
        body,
        mesh=mesh,
        in_specs=placed,
        out_specs=(
            P("fsdp", None),
            P("fsdp", None),
            P("fsdp", None),
            P("fsdp", None),
            P(("rep", "fsdp")),
        ),
        check_vma=False,
    )
```

```python
import functools
import itertools
import jax
import jax.numpy as jnp
from jax import lax
from jax.experimental import pallas as pl
from jax.experimental.pallas import tpu as pltpu
from jax.sharding import PartitionSpec as P

LEN = 192


beta_one = 0.9
beta_two = 0.95
step_count = 20
learn_rate = 0.003
adam_epsilon = 1e-08
blend_rate = 0.6
smoothing = 0.1


def adam_update(gradient, policy, anchor, moment, second):
    moment_new = beta_one * moment + (1.0 - beta_one) * gradient
    second_new = beta_two * second + (1.0 - beta_two) * gradient * gradient
    correct_one = 1.0 - beta_one**step_count
    correct_two = 1.0 - beta_two**step_count
    policy_new = policy - learn_rate * (moment_new / correct_one) / (
        jnp.sqrt(second_new / correct_two) + adam_epsilon
    )
    anchor_new = blend_rate * policy_new + (1.0 - blend_rate) * anchor
    return (policy_new, anchor_new, moment_new, second_new)


def token_scores(values, readout):
    return jnp.sum(jax.nn.log_sigmoid(values * readout[None, :]), axis=1)


def sequence_margin(policy_values, anchor_values, readout, sequence_length):
    token_gap = token_scores(policy_values, readout) - token_scores(anchor_values, readout)
    return jnp.mean(token_gap.reshape(-1, sequence_length), axis=1)


def pair_losses(margins, pair_index, noisy_flags):
    sequence_index = jnp.arange(margins.shape[0], dtype=jnp.int32)
    chosen = jnp.sum(
        jnp.where(pair_index[:, 0:1] == sequence_index[None, :], margins[None, :], 0.0), axis=1
    )
    rejected = jnp.sum(
        jnp.where(pair_index[:, 1:2] == sequence_index[None, :], margins[None, :], 0.0), axis=1
    )
    margin_gap = chosen - rejected
    logit_value = jnp.where(noisy_flags == 1, -margin_gap, margin_gap)
    return -(1.0 - smoothing) * jax.nn.log_sigmoid(logit_value) - smoothing * jax.nn.log_sigmoid(
        -logit_value
    )


def shards(tokens, cotangent, policy, anchor, moment, second, readout, pair_index, noisy_flags):
    part_sum = lax.psum_scatter(
        lax.dot_general(
            tokens, cotangent, (((0,), (0,)), ((), ())), preferred_element_type=jnp.float32
        ),
        "fsdp",
        scatter_dimension=0,
        tiled=True,
    )
    gradient = lax.psum(part_sum.astype(jnp.bfloat16), "rep").astype(jnp.float32)
    policy_next, anchor_next, moment_next, second_next = adam_update(
        gradient, policy, anchor, moment, second
    )
    policy_half = policy_next.astype(jnp.bfloat16)
    anchor_half = anchor_next.astype(jnp.bfloat16)
    policy_whole = lax.all_gather(policy_half, "fsdp", axis=0, tiled=True)
    anchor_whole = lax.all_gather(anchor_half, "fsdp", axis=0, tiled=True)
    policy_values = jnp.dot(tokens, policy_whole, preferred_element_type=jnp.float32)
    anchor_values = jnp.dot(tokens, anchor_whole, preferred_element_type=jnp.float32)
    margins_own = sequence_margin(policy_values, anchor_values, readout, LEN)
    all_margins = lax.all_gather(margins_own, ("rep", "fsdp"), axis=0, tiled=True)
    pair_loss = pair_losses(all_margins, pair_index, noisy_flags)
    return (policy_next, anchor_next, moment_next, second_next, pair_loss)


PLANES = 4
EARLY = 64
MESH_ID = pl.DeviceIdType.MESH


def policy_update(gradient, policy, moment, second):
    moment_new = beta_one * moment + (1.0 - beta_one) * gradient
    second_new = beta_two * second + (1.0 - beta_two) * gradient * gradient
    correct_one = 1.0 - beta_one**step_count
    correct_two = 1.0 - beta_two**step_count
    return policy - learn_rate * (moment_new / correct_one) / (
        jnp.sqrt(second_new / correct_two) + adam_epsilon
    )


def fused_kernel(
    sizes,
    tokens,
    cotangent,
    policy,
    anchor,
    moment,
    second,
    readout,
    pair_index,
    noisy_flags,
    gradient_out,
    loss_out,
    tok,
    cot,
    cot_t,
    anc,
    anc_send,
    par,
    send_a1,
    recv_a1,
    keep_a,
    send_b1,
    recv_b1,
    keep_b,
    send_a2,
    recv_a2,
    send_b2,
    recv_b2,
    send_z,
    recv_z,
    grad_own,
    result,
    weights,
    acc,
    table,
    own_sem,
    tok_sem,
    anc_sem,
    rs_recv,
    xy_recv,
    z_recv,
    out_sem,
    sent_sem,
):
    n, rows, tokens_own, half = sizes
    block = 2 * rows
    span = 4 * block
    pair = 2 * block
    low = half // 2
    me = lax.axis_index("fsdp")
    core = me % 2
    px = (me // 2) % 2
    py = (me // 4) % 2
    pz = me // 8
    chip = me // 2
    mate = me + 1 - 2 * core
    x_mate = me + 2 - 4 * px
    y_mate = me + 4 - 8 * py
    home = chip * block

    top = pz // 2
    near = pz + top * (3 - 2 * pz)
    middle = jnp.logical_and(pz > 0, pz < PLANES - 1)

    def plane(t):
        there = (near, 1 - near, 2, 3)[t]
        return there + top * (3 - 2 * there)

    def z_mate(t):
        return me + 8 * (plane(t) - pz)

    def remote(src, dst, send_sem, recv_sem, device):
        return pltpu.make_async_remote_copy(
            src_ref=src,
            dst_ref=dst,
            send_sem=send_sem,
            recv_sem=recv_sem,
            device_id={"fsdp": device},
            device_id_type=MESH_ID,
        )

    def await_bytes(ref, sem):
        pltpu.make_async_copy(ref, ref, sem).wait()

    barrier = pltpu.get_barrier_semaphore()
    others = [mate, x_mate, y_mate] + [z_mate(t) for t in (1, 2, 3)]
    for other in others:
        pl.semaphore_signal(barrier, inc=1, device_id={"fsdp": other}, device_id_type=MESH_ID)

    mine = pl.ds(pl.multiple_of(core * half, half), half)
    theirs = pl.ds(pl.multiple_of((1 - core) * half, half), half)
    params = (policy, moment, second)

    def columns(i, dy):
        start = plane(3 - i) * span + ((py + dy) % 2) * pair
        return pl.ds(pl.multiple_of(start, pair), pair)

    pieces = [(i, dy) for i in range(PLANES) for dy in (1, 0)]

    for r, side in enumerate((mine, theirs)):
        pltpu.make_async_copy(anchor.at[:, side], anc.at[r], anc_sem.at[r]).start()
    pltpu.make_async_copy(cotangent.at[:, mine], cot.at[core], own_sem.at[0]).start()

    def load(j):
        where = columns(*pieces[j])
        pltpu.make_async_copy(
            tokens.at[:, where], tok.at[core, :, where], tok_sem.at[j]
        ).start()

    load(0)
    load(1)
    pl.semaphore_wait(barrier, len(others))

    unit = half * 2
    sent = {}

    def launch(group, src, dst, recv_sem, device):
        remote(src, dst, sent_sem.at[group], recv_sem, device).start()
        count = 1
        for extent in src.shape:
            count *= extent
        sent[group] = sent.get(group, 0) + count * jnp.dtype(src.dtype).itemsize // unit

    SWAP, REDUCE, SPREAD, POLICY, CHAIN, MARGIN, TOKENS = range(7)

    launch(SWAP, cotangent.at[:, theirs], cot.at[core], own_sem.at[0], mate)
    own_rows = pl.ds(pl.multiple_of(home + core * rows, rows), rows)
    await_bytes(anc.at[0], anc_sem.at[0])
    weights[1, own_rows, :] = anc[0].astype(jnp.bfloat16)

    def chip_at(zz, dy, dx):
        return zz * 4 + ((py + dy) % 2) * 2 + (px + dx) % 2

    kinds = {
        "c": (1, core * (block - EARLY), EARLY),
        "a": (1, (1 - core) * EARLY, block - EARLY),
        "p": (0, 0, block),
    }

    def part(kind, k, which=None):
        m, start, count = kinds[kind]
        if which is not None:
            count = count // 2
            start = start + which * count
        return weights.at[m, pl.ds(pl.multiple_of(k * block + start, 16), count), :]

    def some_rows(count, m=0):
        return weights.at[m, pl.ds(0, count), :]

    def spread(kind, q, zz):
        ref = part(kind, chip_at(zz, 0, 0))
        group = POLICY if kind == "p" else SPREAD
        launch(group, ref, ref, xy_recv.at[q, 0], x_mate)
        launch(group, ref, ref, xy_recv.at[q, 0], y_mate)

    def relay(kind, q, zz):
        await_bytes(some_rows(2 * kinds[kind][2]), xy_recv.at[q, 0])
        group = POLICY if kind == "p" else SPREAD
        ref = part(kind, chip_at(zz, 1, 0), 0)
        launch(group, ref, ref, xy_recv.at[q, 1], x_mate)
        ref = part(kind, chip_at(zz, 0, 1), 1)
        launch(group, ref, ref, xy_recv.at[q, 1], y_mate)

    def relayed(kind, q):
        await_bytes(some_rows(kinds[kind][2]), xy_recv.at[q, 1])

    def z_out(kind, q, k):
        for t in (1, 2, 3):
            ref = part(kind, k)
            launch(SPREAD, ref, ref, z_recv.at[q, pz], z_mate(t))

    def z_in(q, t, count):
        await_bytes(some_rows(count), z_recv.at[q, plane(t)])

    def chain_each(t, act):
        zz = plane(t)
        ref = part("p", chip_at(zz, 0, 0))

        def to(device):
            act(remote(ref, ref, sent_sem.at[CHAIN], z_recv.at[2, zz], device))

        if t < PLANES - 1:
            pl.when(jnp.logical_and(zz <= pz, pz < PLANES - 1))(lambda: to((me + 8) % n))
            pl.when(jnp.logical_and(zz >= pz, pz > 0))(lambda: to((me + n - 8) % n))
        if t == 0:
            pl.when(jnp.logical_not(middle))(lambda: to(z_mate(3)))

    def chain_step(t):
        if t > 0:
            z_in(2, t, block)
        chain_each(t, lambda copy: copy.start())

    spread("c", 8, pz)
    z_out("c", 0, chip)
    await_bytes(anc.at[1], anc_sem.at[1])
    anc_send[...] = anc[1].astype(jnp.bfloat16)
    launch(SWAP, anc_send, weights.at[1, own_rows, :], anc_sem.at[2], mate)
    for j in range(2, len(pieces)):
        load(j)
    for j, key in enumerate(pieces):
        where = columns(*key)
        launch(TOKENS, tokens.at[:, where], tok.at[core, :, where], tok_sem.at[j], mate)
    for a in range(3):
        pltpu.make_async_copy(params[a].at[:, mine], par.at[a, core], own_sem.at[1]).start()
        launch(SWAP, params[a].at[:, theirs], par.at[a, core], own_sem.at[1], mate)

    await_bytes(anc_send, anc_sem.at[2])
    z_out("a", 1, chip)
    spread("a", 0, pz)

    await_bytes(cot, own_sem.at[0])
    for r in range(2):
        cot_t[:, r * tokens_own : (r + 1) * tokens_own] = (
            cot[r].astype(jnp.float32).T.astype(jnp.bfloat16)
        )

    def first(key):
        await_bytes(tok.at[:, :, columns(*key)], tok_sem.at[pieces.index(key)])

    def block_gradient(i, dy, dx):
        target = chip_at(plane(3 - i), dy, dx)
        where = pl.ds(pl.multiple_of(target * block, block), block)
        total = jnp.dot(
            cot_t[:, :tokens_own], tok[0, :, where], preferred_element_type=jnp.float32
        )
        total += jnp.dot(
            cot_t[:, tokens_own:], tok[1, :, where], preferred_element_type=jnp.float32
        )
        if dx == 1:
            send_a1[i, dy] = total[:low].astype(jnp.bfloat16)
        else:
            keep_a[i, dy] = total[:low]
        if dy == 1:
            send_b1[i, dx] = total[low:].astype(jnp.bfloat16)
        else:
            keep_b[i, dx] = total[low:]

    def send_b(i):
        launch(REDUCE, send_b1.at[i], recv_b1.at[i], rs_recv.at[1, i], y_mate)

    def send_a(i):
        launch(REDUCE, send_a1.at[i], recv_a1.at[i], rs_recv.at[0, i], x_mate)

    def stage_one(i, hold=False):
        first((i, 1))
        block_gradient(i, 1, 1)
        block_gradient(i, 1, 0)
        if not hold:
            send_b(i)
        first((i, 0))
        block_gradient(i, 0, 1)
        if not hold:
            send_a(i)
        block_gradient(i, 0, 0)

    def stage_two(i):
        await_bytes(recv_a1.at[i], rs_recv.at[0, i])
        send_a2[i] = (keep_a[i, 1] + recv_a1[i, 1].astype(jnp.float32)).astype(jnp.bfloat16)
        launch(REDUCE, send_a2.at[i], recv_a2.at[i], rs_recv.at[2, i], y_mate)
        await_bytes(recv_b1.at[i], rs_recv.at[1, i])
        send_b2[i] = (keep_b[i, 1] + recv_b1[i, 1].astype(jnp.float32)).astype(jnp.bfloat16)
        launch(REDUCE, send_b2.at[i], recv_b2.at[i], rs_recv.at[3, i], x_mate)

    def stage_three(i):
        await_bytes(recv_a2.at[i], rs_recv.at[2, i])
        total_a = keep_a[i, 0] + recv_a1[i, 0].astype(jnp.float32) + recv_a2[i].astype(jnp.float32)
        await_bytes(recv_b2.at[i], rs_recv.at[3, i])
        total_b = keep_b[i, 0] + recv_b1[i, 0].astype(jnp.float32) + recv_b2[i].astype(jnp.float32)
        if i == PLANES - 1:
            grad_own[:low] = total_a
            grad_own[low:] = total_b
        else:
            send_z[i, :low] = total_a.astype(jnp.bfloat16)
            send_z[i, low:] = total_b.astype(jnp.bfloat16)
            launch(REDUCE, send_z.at[i], recv_z.at[pz], rs_recv.at[4, 0], z_mate(3 - i))

    def anchor_spread(t):
        z_in(1, t, block - EARLY)
        spread("a", t, plane(t))

    def anchor_relay(t):
        relay("a", t, plane(t))

    stage_one(0)
    stage_one(1)
    stage_one(2, hold=True)
    relay("c", 8, pz)
    z_out("c", 0, chip_at(pz, 0, 1))
    stage_two(0)
    send_b(2)
    send_a(2)
    stage_one(3, hold=True)
    stage_two(1)
    stage_three(0)
    anchor_relay(0)
    stage_two(2)
    send_b(3)
    send_a(3)
    stage_three(1)
    anchor_spread(1)
    stage_three(2)
    z_out("c", 0, chip_at(pz, 1, 0))
    stage_two(3)
    anchor_spread(2)
    anchor_relay(1)
    await_bytes(par, own_sem.at[1])
    await_bytes(recv_z.at[pl.ds(0, PLANES - 1)], rs_recv.at[4, 0])
    stage_three(3)
    gradient = grad_own[...]
    for t in (1, 2, 3):
        gradient += recv_z[plane(t)].astype(jnp.float32)
    gradient = gradient.T
    for r in range(2):
        own = gradient[r * rows : (r + 1) * rows]
        updated = policy_update(own, par[0, r], par[1, r], par[2, r])
        result[r] = own
        weights[0, pl.ds(pl.multiple_of(home + r * rows, rows), rows), :] = updated.astype(
            jnp.bfloat16
        )
    chain_step(0)
    spread("p", 4, pz)

    tile = tokens_own
    scale = readout[core]

    def score_sum(values):
        low_part = jnp.minimum(values, 0.0).reshape(LEN // 8, 8, half)
        factor = (1.0 + jnp.exp(-jnp.abs(values))).reshape(LEN // 8, 8, half)
        product = factor[0]
        for j in range(1, LEN // 8):
            product = product * factor[j]
        return jnp.sum(low_part, axis=0) - jnp.log(product)

    def multiply(m, t):
        where = pl.ds(pl.multiple_of(plane(t) * span, span), span)

        @pl.loop(0, 2)
        def _(i):
            value = jnp.dot(
                tok[i, :, where], weights[m, where, :], preferred_element_type=jnp.float32
            )
            acc[m, i] = value if t == 0 else acc[m, i] + value

    def anchor_multiply(t):
        relayed("a", t)
        if t > 0:
            z_in(0, t, 4 * EARLY)
        multiply(1, t)

    def policy_multiply(t):
        relayed("p", 4 + t)
        multiply(0, t)

    def policy_spread(t):
        spread("p", 4 + t, plane(t))

    def policy_relay(t):
        relay("p", 4 + t, plane(t))

    def spot(zz, dy, dx):
        return pl.ds(pl.multiple_of(chip_at(zz, dy, dx) * block, block), block)

    def compute_near(zz):
        @pl.loop(0, 2)
        def _(i):
            value = acc[0, i]
            for dy, dx in ((0, 0), (0, 1), (1, 0)):
                where = spot(zz, dy, dx)
                value += jnp.dot(
                    tok[i, :, where], weights[0, where, :], preferred_element_type=jnp.float32
                )
            acc[0, i] = value

    def compute_last(zz):
        where = spot(zz, 1, 1)

        @pl.loop(0, 2)
        def _(i):
            value = acc[0, i] + jnp.dot(
                tok[i, :, where], weights[0, where, :], preferred_element_type=jnp.float32
            )
            acc[1, i] = (blend_rate * value + (1.0 - blend_rate) * acc[1, i]) * scale
            acc[0, i] = value * scale
            for j in range(tile // LEN):
                gap = score_sum(acc[0, i, j * LEN : (j + 1) * LEN]) - score_sum(
                    acc[1, i, j * LEN : (j + 1) * LEN]
                )
                gap = jnp.sum(gap, axis=0, keepdims=True)
                gap = jnp.sum(gap, axis=1, keepdims=True)
                table[me, pl.ds(i * (tile // LEN) + j, 1), :] = jnp.broadcast_to(
                    gap * (1.0 / LEN), (1, 128)
                )

    pltpu.make_async_copy(result.at[core], gradient_out.at[:, mine], out_sem.at[0]).start()
    launch(REDUCE, result.at[1 - core], gradient_out.at[:, mine], out_sem.at[0], mate)

    anchor_spread(3)
    relayed("c", 8)
    anchor_multiply(0)
    anchor_relay(2)
    policy_relay(0)
    chain_step(1)

    @pl.when(middle)
    def _():
        chain_step(2)

    policy_spread(1)
    z_out("c", 0, chip_at(pz, 1, 1))
    anchor_relay(3)
    policy_multiply(0)

    @pl.when(jnp.logical_not(middle))
    def _():
        chain_step(2)

    chain_step(3)
    policy_spread(2)
    policy_relay(1)
    policy_spread(3)
    anchor_multiply(1)
    anchor_multiply(2)
    policy_relay(2)
    anchor_multiply(3)
    policy_multiply(1)
    policy_relay(3)
    compute_near(plane(3))
    policy_multiply(2)
    await_bytes(gradient_out, out_sem.at[0])
    await_bytes(tok.at[0], sent_sem.at[TOKENS])
    for group in (SWAP, REDUCE, SPREAD, POLICY):
        await_bytes(some_rows(sent[group]), sent_sem.at[group])
    pl.when(middle)(lambda: await_bytes(some_rows(4 * block), sent_sem.at[CHAIN]))
    pl.when(jnp.logical_not(middle))(lambda: await_bytes(some_rows(2 * block), sent_sem.at[CHAIN]))
    relayed("p", 7)
    compute_last(plane(3))

    everyone = [
        (t, dy, dx, dc) for t in (3, 2, 1, 0) for dy, dx, dc in itertools.product((1, 0), repeat=3)
    ][:-1]
    for t, dy, dx, dc in everyone:
        there = chip_at(plane(t), dy, dx) * 2 + (core + dc) % 2
        ref = table.at[me]
        remote(ref, ref, sent_sem.at[MARGIN], out_sem.at[1], there).start()
    await_bytes(table.at[pl.ds(0, n - 1)], out_sem.at[1])
    await_bytes(table.at[pl.ds(0, n - 1)], sent_sem.at[MARGIN])
    margins = table[...].reshape(n // 2, 2, -1, 128)
    margins = (margins[:, 0] + margins[:, 1]).reshape(-1, 128)
    sequence = lax.broadcasted_iota(jnp.int32, margins.shape, 0)

    def margin_of(index):
        return jnp.sum(jnp.where(sequence == index, margins, 0.0), axis=0, keepdims=True)

    for p in range(noisy_flags.shape[0]):
        gap = margin_of(pair_index[p, 0]) - margin_of(pair_index[p, 1])
        gap = jnp.where(noisy_flags[p] == 1, -gap, gap)
        tail = jnp.log(1.0 + jnp.exp(-jnp.abs(gap)))
        loss = (1.0 - smoothing) * (tail - jnp.minimum(gap, 0.0)) + smoothing * (
            tail + jnp.maximum(gap, 0.0)
        )
        loss_out[p] = loss[0, 0]


def finish_kernel(
    gradient,
    policy,
    anchor,
    moment,
    second,
    loss,
    policy_out,
    anchor_out,
    moment_out,
    second_out,
    loss_out,
):
    updated = adam_update(gradient[...], policy[...], anchor[...], moment[...], second[...])
    for out, value in zip((policy_out, anchor_out, moment_out, second_out), updated):
        out[...] = value
    for p in range(loss.shape[0]):
        loss_out[p] = loss[p]


def fused_shards(n, tokens, cotangent, policy, anchor, moment, second, readout, pair_index, noisy_flags):
    tokens_own, depth = tokens.shape
    rows, channels = policy.shape
    half = channels // 2
    block = 2 * rows
    low = half // 2
    sizes = (n, rows, tokens_own, half)
    bf, f32 = jnp.bfloat16, jnp.float32
    vmem, dma = pltpu.VMEM, pltpu.SemaphoreType.DMA
    hbm = pl.BlockSpec(memory_space=pl.ANY)
    whole = pl.BlockSpec(memory_space=pltpu.VMEM)
    smem = pl.BlockSpec(memory_space=pltpu.SMEM)
    weight = jax.ShapeDtypeStruct((rows, channels), f32)
    losses = jax.ShapeDtypeStruct(noisy_flags.shape, f32)
    gradient, loss = pl.pallas_call(
        functools.partial(fused_kernel, sizes),
        out_shape=(weight, losses),
        in_specs=[hbm] * 6 + [whole] + [smem] * 2,
        out_specs=(hbm, smem),
        scratch_shapes=[
            vmem((2, tokens_own, depth), bf),
            vmem((2, tokens_own, half), bf),
            vmem((half, 2 * tokens_own), bf),
            vmem((2, rows, half), f32),
            vmem((rows, half), bf),
            vmem((3, 2, rows, half), f32),
            vmem((4, 2, low, block), bf),
            vmem((4, 2, low, block), bf),
            vmem((4, 2, low, block), f32),
            vmem((4, 2, low, block), bf),
            vmem((4, 2, low, block), bf),
            vmem((4, 2, low, block), f32),
            vmem((4, low, block), bf),
            vmem((4, low, block), bf),
            vmem((4, low, block), bf),
            vmem((4, low, block), bf),
            vmem((3, half, block), bf),
            vmem((4, half, block), bf),
            vmem((half, block), f32),
            vmem((2, rows, half), f32),
            vmem((2, depth, half), bf),
            vmem((2, 2, tokens_own, half), f32),
            vmem((n, 2 * tokens_own // LEN, 128), f32),
            dma((2,)),
            dma((8,)),
            dma((3,)),
            dma((5, 4)),
            dma((9, 2)),
            dma((3, 4)),
            dma((2,)),
            dma((7,)),
        ],
        compiler_params=pltpu.CompilerParams(
            collective_id=0, has_side_effects=True, vmem_limit_bytes=56 * 1024 * 1024
        ),
    )(
        tokens,
        cotangent,
        policy,
        anchor,
        moment,
        second,
        readout.reshape(2, 1, half),
        pair_index,
        noisy_flags,
    )
    policy_next, anchor_next, moment_next, second_next, pair_loss = pl.pallas_call(
        finish_kernel,
        out_shape=(weight,) * 4 + (losses,),
        in_specs=[whole] * 5 + [smem],
        out_specs=(whole,) * 4 + (smem,),
    )(gradient, policy, anchor, moment, second, loss)
    return (policy_next, anchor_next, moment_next, second_next, pair_loss)


def solution(mesh):
    placed = (
        P(("rep", "fsdp"), None),
        P(("rep", "fsdp"), None),
        P("fsdp", None),
        P("fsdp", None),
        P("fsdp", None),
        P("fsdp", None),
        P(),
        P(("rep", "fsdp"), None),
        P(("rep", "fsdp")),
    )
    n = mesh.shape["fsdp"]
    body = shards
    if mesh.shape["rep"] == 1 and n == 8 * PLANES:
        body = functools.partial(fused_shards, n)
    return jax.shard_map(
        body,
        mesh=mesh,
        in_specs=placed,
        out_specs=(
            P("fsdp", None),
            P("fsdp", None),
            P("fsdp", None),
            P("fsdp", None),
            P(("rep", "fsdp")),
        ),
        check_vma=False,
    )
```

```python
import functools
import itertools
import jax
import jax.numpy as jnp
from jax import lax
from jax.experimental import pallas as pl
from jax.experimental.pallas import tpu as pltpu
from jax.sharding import PartitionSpec as P

LEN = 192


beta_one = 0.9
beta_two = 0.95
step_count = 20
learn_rate = 0.003
adam_epsilon = 1e-08
blend_rate = 0.6
smoothing = 0.1


def adam_update(gradient, policy, anchor, moment, second):
    moment_new = beta_one * moment + (1.0 - beta_one) * gradient
    second_new = beta_two * second + (1.0 - beta_two) * gradient * gradient
    correct_one = 1.0 - beta_one**step_count
    correct_two = 1.0 - beta_two**step_count
    policy_new = policy - learn_rate * (moment_new / correct_one) / (
        jnp.sqrt(second_new / correct_two) + adam_epsilon
    )
    anchor_new = blend_rate * policy_new + (1.0 - blend_rate) * anchor
    return (policy_new, anchor_new, moment_new, second_new)


def token_scores(values, readout):
    return jnp.sum(jax.nn.log_sigmoid(values * readout[None, :]), axis=1)


def sequence_margin(policy_values, anchor_values, readout, sequence_length):
    token_gap = token_scores(policy_values, readout) - token_scores(anchor_values, readout)
    return jnp.mean(token_gap.reshape(-1, sequence_length), axis=1)


def pair_losses(margins, pair_index, noisy_flags):
    sequence_index = jnp.arange(margins.shape[0], dtype=jnp.int32)
    chosen = jnp.sum(
        jnp.where(pair_index[:, 0:1] == sequence_index[None, :], margins[None, :], 0.0), axis=1
    )
    rejected = jnp.sum(
        jnp.where(pair_index[:, 1:2] == sequence_index[None, :], margins[None, :], 0.0), axis=1
    )
    margin_gap = chosen - rejected
    logit_value = jnp.where(noisy_flags == 1, -margin_gap, margin_gap)
    return -(1.0 - smoothing) * jax.nn.log_sigmoid(logit_value) - smoothing * jax.nn.log_sigmoid(
        -logit_value
    )


def shards(tokens, cotangent, policy, anchor, moment, second, readout, pair_index, noisy_flags):
    part_sum = lax.psum_scatter(
        lax.dot_general(
            tokens, cotangent, (((0,), (0,)), ((), ())), preferred_element_type=jnp.float32
        ),
        "fsdp",
        scatter_dimension=0,
        tiled=True,
    )
    gradient = lax.psum(part_sum.astype(jnp.bfloat16), "rep").astype(jnp.float32)
    policy_next, anchor_next, moment_next, second_next = adam_update(
        gradient, policy, anchor, moment, second
    )
    policy_half = policy_next.astype(jnp.bfloat16)
    anchor_half = anchor_next.astype(jnp.bfloat16)
    policy_whole = lax.all_gather(policy_half, "fsdp", axis=0, tiled=True)
    anchor_whole = lax.all_gather(anchor_half, "fsdp", axis=0, tiled=True)
    policy_values = jnp.dot(tokens, policy_whole, preferred_element_type=jnp.float32)
    anchor_values = jnp.dot(tokens, anchor_whole, preferred_element_type=jnp.float32)
    margins_own = sequence_margin(policy_values, anchor_values, readout, LEN)
    all_margins = lax.all_gather(margins_own, ("rep", "fsdp"), axis=0, tiled=True)
    pair_loss = pair_losses(all_margins, pair_index, noisy_flags)
    return (policy_next, anchor_next, moment_next, second_next, pair_loss)


LOG2E = 1.4426950408889634
PLANES = 4
MESH_ID = pl.DeviceIdType.MESH


def policy_update(gradient, policy, moment, second):
    moment_new = beta_one * moment + (1.0 - beta_one) * gradient
    second_new = beta_two * second + (1.0 - beta_two) * gradient * gradient
    correct_one = 1.0 - beta_one**step_count
    correct_two = 1.0 - beta_two**step_count
    return policy - learn_rate * (moment_new / correct_one) / (
        jnp.sqrt(second_new / correct_two) + adam_epsilon
    )


def fused_kernel(
    sizes,
    tokens,
    cotangent,
    policy,
    anchor,
    moment,
    second,
    readout,
    pair_index,
    noisy_flags,
    gradient_out,
    loss_out,
    tok,
    cot,
    cot_t,
    anc,
    anc_send,
    par,
    send_a1,
    recv_a1,
    keep_a,
    send_b1,
    recv_b1,
    keep_b,
    send_a2,
    recv_a2,
    send_b2,
    recv_b2,
    send_z,
    recv_z,
    grad_own,
    result,
    weights,
    acc,
    table,
    own_sem,
    tok_sem,
    anc_sem,
    rs_recv,
    xy_recv,
    z_recv,
    out_sem,
    sent_sem,
):
    n, rows, tokens_own, half = sizes
    block = 2 * rows
    span = 4 * block
    pair = 2 * block
    low = half // 2
    me = lax.axis_index("fsdp")
    core = me % 2
    px = (me // 2) % 2
    py = (me // 4) % 2
    pz = me // 8
    chip = me // 2
    mate = me + 1 - 2 * core
    x_mate = me + 2 - 4 * px
    y_mate = me + 4 - 8 * py
    home = chip * block

    top = pz // 2
    near = pz + top * (3 - 2 * pz)
    middle = jnp.logical_and(pz > 0, pz < PLANES - 1)

    def plane(t):
        there = (near, 1 - near, 2, 3)[t]
        return there + top * (3 - 2 * there)

    def z_mate(t):
        return me + 8 * (plane(t) - pz)

    def remote(src, dst, send_sem, recv_sem, device):
        return pltpu.make_async_remote_copy(
            src_ref=src,
            dst_ref=dst,
            send_sem=send_sem,
            recv_sem=recv_sem,
            device_id={"fsdp": device},
            device_id_type=MESH_ID,
        )

    def await_bytes(ref, sem):
        pltpu.make_async_copy(ref, ref, sem).wait()

    barrier = pltpu.get_barrier_semaphore()
    others = [mate, x_mate, y_mate] + [z_mate(t) for t in (1, 2, 3)]
    for other in others:
        pl.semaphore_signal(barrier, inc=1, device_id={"fsdp": other}, device_id_type=MESH_ID)

    mine = pl.ds(pl.multiple_of(core * half, half), half)
    theirs = pl.ds(pl.multiple_of((1 - core) * half, half), half)
    params = (policy, moment, second)

    def columns(i, dy):
        start = plane(3 - i) * span + ((py + dy) % 2) * pair
        return pl.ds(pl.multiple_of(start, pair), pair)

    pieces = [(i, dy) for i in range(PLANES) for dy in (1, 0)]

    for r, side in enumerate((mine, theirs)):
        pltpu.make_async_copy(anchor.at[:, side], anc.at[r], anc_sem.at[r]).start()
    pltpu.make_async_copy(cotangent.at[:, mine], cot.at[core], own_sem.at[0]).start()

    def load(j):
        where = columns(*pieces[j])
        pltpu.make_async_copy(
            tokens.at[:, where], tok.at[core, :, where], tok_sem.at[j]
        ).start()

    load(0)
    load(1)
    pl.semaphore_wait(barrier, len(others))

    unit = half * 2
    sent = {}

    def launch(group, src, dst, recv_sem, device):
        remote(src, dst, sent_sem.at[group], recv_sem, device).start()
        count = 1
        for extent in src.shape:
            count *= extent
        sent[group] = sent.get(group, 0) + count * jnp.dtype(src.dtype).itemsize // unit

    SWAP, REDUCE, SPREAD, POLICY, CHAIN, MARGIN, TOKENS = range(7)

    launch(SWAP, cotangent.at[:, theirs], cot.at[core], own_sem.at[0], mate)
    own_rows = pl.ds(pl.multiple_of(home + core * rows, rows), rows)
    await_bytes(anc.at[1], anc_sem.at[1])
    anc_send[...] = anc[1].astype(jnp.bfloat16)
    launch(SWAP, anc_send, weights.at[1, own_rows, :], anc_sem.at[2], mate)
    await_bytes(anc.at[0], anc_sem.at[0])
    weights[1, own_rows, :] = anc[0].astype(jnp.bfloat16)

    def chip_at(zz, dy, dx):
        return zz * 4 + ((py + dy) % 2) * 2 + (px + dx) % 2

    kinds = {
        "a": (1, 0, block),
        "p": (0, 0, block),
    }

    def part(kind, k, which=None):
        m, start, count = kinds[kind]
        if which is not None:
            count = count // 2
            start = start + which * count
        return weights.at[m, pl.ds(pl.multiple_of(k * block + start, 16), count), :]

    def some_rows(count, m=0):
        return weights.at[m, pl.ds(0, count), :]

    def spread(kind, q, zz):
        ref = part(kind, chip_at(zz, 0, 0))
        group = POLICY if kind == "p" else SPREAD
        launch(group, ref, ref, xy_recv.at[q, 0], x_mate)
        launch(group, ref, ref, xy_recv.at[q, 0], y_mate)

    def relay(kind, q, zz):
        await_bytes(some_rows(2 * kinds[kind][2]), xy_recv.at[q, 0])
        forward(kind, q, zz)

    def forward(kind, q, zz):
        group = POLICY if kind == "p" else SPREAD
        ref = part(kind, chip_at(zz, 1, 0), 0)
        launch(group, ref, ref, xy_recv.at[q, 1], x_mate)
        ref = part(kind, chip_at(zz, 0, 1), 1)
        launch(group, ref, ref, xy_recv.at[q, 1], y_mate)

    def relayed(kind, q):
        await_bytes(some_rows(kinds[kind][2]), xy_recv.at[q, 1])

    def z_out(kind, q, k):
        for t in (1, 2, 3):
            ref = part(kind, k)
            launch(SPREAD, ref, ref, z_recv.at[q, pz], z_mate(t))

    def beside(kind, q, dy, dx):
        ref = part(kind, chip_at(pz, dy, dx))
        group = POLICY if kind == "p" else SPREAD
        launch(group, ref, ref, z_recv.at[q, 0], z_mate(1))

    def z_in(q, t, count):
        await_bytes(some_rows(count), z_recv.at[q, plane(t)])

    def chain_each(t, act):
        zz = plane(t)
        ref = part("p", chip_at(zz, 0, 0))

        def to(device):
            act(remote(ref, ref, sent_sem.at[CHAIN], z_recv.at[2, zz], device))

        if t < PLANES - 1:
            pl.when(jnp.logical_and(zz <= pz, pz < PLANES - 1))(lambda: to((me + 8) % n))
            pl.when(jnp.logical_and(zz >= pz, pz > 0))(lambda: to((me + n - 8) % n))
        if t == 0:
            pl.when(jnp.logical_not(middle))(lambda: to(z_mate(3)))

    def chain_step(t):
        if t > 0:
            z_in(2, t, block)
        chain_each(t, lambda copy: copy.start())

    for j in range(2, len(pieces)):
        load(j)
    for j, key in enumerate(pieces):
        where = columns(*key)
        launch(TOKENS, tokens.at[:, where], tok.at[core, :, where], tok_sem.at[j], mate)
    for a in range(3):
        pltpu.make_async_copy(params[a].at[:, mine], par.at[a, core], own_sem.at[1]).start()
        launch(SWAP, params[a].at[:, theirs], par.at[a, core], own_sem.at[1], mate)

    await_bytes(anc_send, anc_sem.at[2])
    z_out("a", 1, chip)
    spread("a", 0, pz)

    await_bytes(cot, own_sem.at[0])
    for r in range(2):
        cot_t[:, r * tokens_own : (r + 1) * tokens_own] = (
            cot[r].astype(jnp.float32).T.astype(jnp.bfloat16)
        )

    def first(key):
        await_bytes(tok.at[:, :, columns(*key)], tok_sem.at[pieces.index(key)])

    def block_gradient(i, dy, dx):
        target = chip_at(plane(3 - i), dy, dx)
        where = pl.ds(pl.multiple_of(target * block, block), block)
        total = jnp.dot(
            cot_t[:, :tokens_own], tok[0, :, where], preferred_element_type=jnp.float32
        )
        total += jnp.dot(
            cot_t[:, tokens_own:], tok[1, :, where], preferred_element_type=jnp.float32
        )
        if dx == 1:
            send_a1[i, dy] = total[:low].astype(jnp.bfloat16)
        else:
            keep_a[i, dy] = total[:low]
        if dy == 1:
            send_b1[i, dx] = total[low:].astype(jnp.bfloat16)
        else:
            keep_b[i, dx] = total[low:]

    def send_b(*at):
        launch(REDUCE, send_b1.at[at], recv_b1.at[at], rs_recv.at[1, at[0]], y_mate)

    def send_a(*at):
        launch(REDUCE, send_a1.at[at], recv_a1.at[at], rs_recv.at[0, at[0]], x_mate)

    def stage_one(i, hold=False):
        first((i, 1))
        block_gradient(i, 1, 1)
        if not hold:
            send_a(i, 1)
            send_b(i, 1)
        block_gradient(i, 1, 0)
        if not hold:
            send_b(i, 0)
        first((i, 0))
        block_gradient(i, 0, 1)
        if not hold:
            send_a(i, 0)
        block_gradient(i, 0, 0)

    def stage_two(i):
        await_bytes(recv_a1.at[i], rs_recv.at[0, i])
        send_a2[i] = (keep_a[i, 1] + recv_a1[i, 1].astype(jnp.float32)).astype(jnp.bfloat16)
        launch(REDUCE, send_a2.at[i], recv_a2.at[i], rs_recv.at[2, i], y_mate)
        await_bytes(recv_b1.at[i], rs_recv.at[1, i])
        send_b2[i] = (keep_b[i, 1] + recv_b1[i, 1].astype(jnp.float32)).astype(jnp.bfloat16)
        launch(REDUCE, send_b2.at[i], recv_b2.at[i], rs_recv.at[3, i], x_mate)

    def stage_three(i):
        await_bytes(recv_a2.at[i], rs_recv.at[2, i])
        total_a = keep_a[i, 0] + recv_a1[i, 0].astype(jnp.float32) + recv_a2[i].astype(jnp.float32)
        await_bytes(recv_b2.at[i], rs_recv.at[3, i])
        total_b = keep_b[i, 0] + recv_b1[i, 0].astype(jnp.float32) + recv_b2[i].astype(jnp.float32)
        if i == PLANES - 1:
            grad_own[:low] = total_a
            grad_own[low:] = total_b
        else:
            send_z[i, :low] = total_a.astype(jnp.bfloat16)
            send_z[i, low:] = total_b.astype(jnp.bfloat16)
            launch(REDUCE, send_z.at[i], recv_z.at[pz], rs_recv.at[4, 0], z_mate(3 - i))

    def anchor_spread(t):
        z_in(1, t, block)
        spread("a", t, plane(t))

    def anchor_relay(t):
        relay("a", t, plane(t))

    stage_one(0)
    stage_one(1)
    stage_one(2, hold=True)
    stage_two(0)
    send_b(2)
    send_a(2)
    await_bytes(some_rows(2 * block, 1), xy_recv.at[0, 0])
    beside("a", 0, 0, 1)
    stage_one(3, hold=True)
    stage_two(1)
    stage_three(0)
    beside("a", 0, 1, 0)
    forward("a", 0, pz)
    stage_two(2)
    send_b(3)
    send_a(3)
    stage_three(1)
    anchor_spread(2)
    stage_three(2)
    relayed("a", 0)
    beside("a", 0, 1, 1)
    stage_two(3)
    anchor_relay(2)
    await_bytes(par, own_sem.at[1])
    await_bytes(recv_z.at[pl.ds(0, PLANES - 1)], rs_recv.at[4, 0])
    stage_three(3)
    gradient = grad_own[...]
    for t in (1, 2, 3):
        gradient += recv_z[plane(t)].astype(jnp.float32)
    gradient = gradient.T
    for r in range(2):
        own = gradient[r * rows : (r + 1) * rows]
        updated = policy_update(own, par[0, r], par[1, r], par[2, r])
        result[r] = own
        weights[0, pl.ds(pl.multiple_of(home + r * rows, rows), rows), :] = updated.astype(
            jnp.bfloat16
        )
    chain_step(0)
    spread("p", 4, pz)

    tile = tokens_own
    scale = readout[core] * LOG2E
    blend_scale = scale * blend_rate
    anchor_scale = scale * (1.0 - blend_rate)

    def score_sum(values):
        low_part = jnp.minimum(values, 0.0).reshape(LEN // 8, 8, half)
        factor = (1.0 + jnp.exp2(-jnp.abs(values))).reshape(LEN // 8, 8, half)
        product = factor[0]
        for j in range(1, LEN // 8):
            product = product * factor[j]
        return jnp.sum(low_part, axis=0) - jnp.log2(product)

    def multiply(m, zz, t):
        where = pl.ds(pl.multiple_of(zz * span, span), span)

        @pl.loop(0, 2)
        def _(i):
            value = jnp.dot(
                tok[i, :, where], weights[m, where, :], preferred_element_type=jnp.float32
            )
            value = value if t == 0 else acc[m, i] + value
            acc[m, i] = value * anchor_scale if m == 1 and t == PLANES - 1 else value

    def anchor_multiply(t):
        if t == 1:
            z_in(1, 1, block)
            await_bytes(some_rows(3 * block), z_recv.at[0, 0])
        elif t > 1:
            relayed("a", t)
        multiply(1, plane(t), t)

    first_plane = jnp.where(middle, plane(2), plane(3))
    last_plane = jnp.where(middle, plane(3), plane(2))

    def spot(zz, dy, dx):
        return pl.ds(pl.multiple_of(chip_at(zz, dy, dx) * block, block), block)

    def compute_near(zz):
        @pl.loop(0, 2)
        def _(i):
            value = acc[0, i]
            for dy, dx in ((0, 0), (0, 1), (1, 0)):
                where = spot(zz, dy, dx)
                value += jnp.dot(
                    tok[i, :, where], weights[0, where, :], preferred_element_type=jnp.float32
                )
            acc[0, i] = value

    def compute_last(zz):
        where = spot(zz, 1, 1)

        @pl.loop(0, 2)
        def _(i):
            value = acc[0, i] + jnp.dot(
                tok[i, :, where], weights[0, where, :], preferred_element_type=jnp.float32
            )
            acc[1, i] = value * blend_scale + acc[1, i]
            acc[0, i] = value * scale
            for j in range(tile // LEN):
                gap = score_sum(acc[0, i, j * LEN : (j + 1) * LEN]) - score_sum(
                    acc[1, i, j * LEN : (j + 1) * LEN]
                )
                gap = jnp.sum(gap, axis=0, keepdims=True)
                gap = jnp.sum(gap, axis=1, keepdims=True)
                table[me, pl.ds(i * (tile // LEN) + j, 1), :] = jnp.broadcast_to(
                    gap * (1.0 / (LEN * LOG2E)), (1, 128)
                )

    pltpu.make_async_copy(result.at[core], gradient_out.at[:, mine], out_sem.at[0]).start()
    launch(REDUCE, result.at[1 - core], gradient_out.at[:, mine], out_sem.at[0], mate)

    anchor_spread(3)
    anchor_multiply(0)
    relay("p", 4, pz)

    @pl.when(middle)
    def _():
        chain_step(1)
        chain_step(2)

    beside("p", 3, 0, 1)
    beside("p", 3, 1, 0)
    anchor_multiply(2)
    anchor_relay(3)
    pl.when(jnp.logical_not(middle))(lambda: chain_step(3))
    spread("p", 5, first_plane)
    relayed("p", 4)
    beside("p", 3, 1, 1)
    multiply(0, pz, 0)

    @pl.when(middle)
    def _():
        chain_step(3)

    @pl.when(jnp.logical_not(middle))
    def _():
        chain_step(2)

    spread("p", 6, last_plane)
    anchor_multiply(1)
    relay("p", 5, first_plane)
    anchor_multiply(3)
    relay("p", 6, last_plane)
    relayed("p", 5)
    multiply(0, first_plane, 2)
    pl.when(jnp.logical_not(middle))(lambda: chain_step(1))
    await_bytes(some_rows(3 * block), z_recv.at[3, 0])
    multiply(0, plane(1), 1)
    compute_near(last_plane)
    await_bytes(gradient_out, out_sem.at[0])
    await_bytes(tok.at[0], sent_sem.at[TOKENS])
    for group in (SWAP, REDUCE, SPREAD, POLICY):
        await_bytes(some_rows(sent[group]), sent_sem.at[group])
    pl.when(middle)(lambda: await_bytes(some_rows(4 * block), sent_sem.at[CHAIN]))
    pl.when(jnp.logical_not(middle))(lambda: await_bytes(some_rows(2 * block), sent_sem.at[CHAIN]))
    relayed("p", 6)
    compute_last(last_plane)

    everyone = [
        (t, dy, dx, dc) for t in (3, 2, 1, 0) for dy, dx, dc in itertools.product((1, 0), repeat=3)
    ][:-1]
    for t, dy, dx, dc in everyone:
        there = chip_at(plane(t), dy, dx) * 2 + (core + dc) % 2
        ref = table.at[me]
        remote(ref, ref, sent_sem.at[MARGIN], out_sem.at[1], there).start()
    await_bytes(table.at[pl.ds(0, n - 1)], out_sem.at[1])
    await_bytes(table.at[pl.ds(0, n - 1)], sent_sem.at[MARGIN])
    margins = table[...].reshape(n // 2, 2, -1, 128)
    margins = (margins[:, 0] + margins[:, 1]).reshape(-1, 128)
    sequence = lax.broadcasted_iota(jnp.int32, margins.shape, 0)

    def margin_of(index):
        return jnp.sum(jnp.where(sequence == index, margins, 0.0), axis=0, keepdims=True)

    for p in range(noisy_flags.shape[0]):
        gap = margin_of(pair_index[p, 0]) - margin_of(pair_index[p, 1])
        gap = jnp.where(noisy_flags[p] == 1, -gap, gap)
        tail = jnp.log(1.0 + jnp.exp(-jnp.abs(gap)))
        loss = (1.0 - smoothing) * (tail - jnp.minimum(gap, 0.0)) + smoothing * (
            tail + jnp.maximum(gap, 0.0)
        )
        loss_out[p] = loss[0, 0]


def finish_kernel(
    gradient,
    policy,
    anchor,
    moment,
    second,
    loss,
    policy_out,
    anchor_out,
    moment_out,
    second_out,
    loss_out,
):
    updated = adam_update(gradient[...], policy[...], anchor[...], moment[...], second[...])
    for out, value in zip((policy_out, anchor_out, moment_out, second_out), updated):
        out[...] = value
    for p in range(loss.shape[0]):
        loss_out[p] = loss[p]


def fused_shards(n, tokens, cotangent, policy, anchor, moment, second, readout, pair_index, noisy_flags):
    tokens_own, depth = tokens.shape
    rows, channels = policy.shape
    half = channels // 2
    block = 2 * rows
    low = half // 2
    sizes = (n, rows, tokens_own, half)
    bf, f32 = jnp.bfloat16, jnp.float32
    vmem, dma = pltpu.VMEM, pltpu.SemaphoreType.DMA
    hbm = pl.BlockSpec(memory_space=pl.ANY)
    whole = pl.BlockSpec(memory_space=pltpu.VMEM)
    smem = pl.BlockSpec(memory_space=pltpu.SMEM)
    weight = jax.ShapeDtypeStruct((rows, channels), f32)
    losses = jax.ShapeDtypeStruct(noisy_flags.shape, f32)
    gradient, loss = pl.pallas_call(
        functools.partial(fused_kernel, sizes),
        out_shape=(weight, losses),
        in_specs=[hbm] * 6 + [whole] + [smem] * 2,
        out_specs=(hbm, smem),
        scratch_shapes=[
            vmem((2, tokens_own, depth), bf),
            vmem((2, tokens_own, half), bf),
            vmem((half, 2 * tokens_own), bf),
            vmem((2, rows, half), f32),
            vmem((rows, half), bf),
            vmem((3, 2, rows, half), f32),
            vmem((4, 2, low, block), bf),
            vmem((4, 2, low, block), bf),
            vmem((4, 2, low, block), f32),
            vmem((4, 2, low, block), bf),
            vmem((4, 2, low, block), bf),
            vmem((4, 2, low, block), f32),
            vmem((4, low, block), bf),
            vmem((4, low, block), bf),
            vmem((4, low, block), bf),
            vmem((4, low, block), bf),
            vmem((3, half, block), bf),
            vmem((4, half, block), bf),
            vmem((half, block), f32),
            vmem((2, rows, half), f32),
            vmem((2, depth, half), bf),
            vmem((2, 2, tokens_own, half), f32),
            vmem((n, 2 * tokens_own // LEN, 128), f32),
            dma((2,)),
            dma((8,)),
            dma((3,)),
            dma((5, 4)),
            dma((7, 2)),
            dma((4, 4)),
            dma((2,)),
            dma((7,)),
        ],
        compiler_params=pltpu.CompilerParams(
            collective_id=0, has_side_effects=True, vmem_limit_bytes=56 * 1024 * 1024
        ),
    )(
        tokens,
        cotangent,
        policy,
        anchor,
        moment,
        second,
        readout.reshape(2, 1, half),
        pair_index,
        noisy_flags,
    )
    policy_next, anchor_next, moment_next, second_next, pair_loss = pl.pallas_call(
        finish_kernel,
        out_shape=(weight,) * 4 + (losses,),
        in_specs=[whole] * 5 + [smem],
        out_specs=(whole,) * 4 + (smem,),
    )(gradient, policy, anchor, moment, second, loss)
    return (policy_next, anchor_next, moment_next, second_next, pair_loss)


def solution(mesh):
    placed = (
        P(("rep", "fsdp"), None),
        P(("rep", "fsdp"), None),
        P("fsdp", None),
        P("fsdp", None),
        P("fsdp", None),
        P("fsdp", None),
        P(),
        P(("rep", "fsdp"), None),
        P(("rep", "fsdp")),
    )
    n = mesh.shape["fsdp"]
    body = shards
    if mesh.shape["rep"] == 1 and n == 8 * PLANES:
        body = functools.partial(fused_shards, n)
    return jax.shard_map(
        body,
        mesh=mesh,
        in_specs=placed,
        out_specs=(
            P("fsdp", None),
            P("fsdp", None),
            P("fsdp", None),
            P("fsdp", None),
            P(("rep", "fsdp")),
        ),
        check_vma=False,
    )
```

```python
import functools
import itertools
import jax
import jax.numpy as jnp
from jax import lax
from jax.experimental import pallas as pl
from jax.experimental.pallas import tpu as pltpu
from jax.sharding import PartitionSpec as P

LEN = 192


beta_one = 0.9
beta_two = 0.95
step_count = 20
learn_rate = 0.003
adam_epsilon = 1e-08
blend_rate = 0.6
smoothing = 0.1


def adam_update(gradient, policy, anchor, moment, second):
    moment_new = beta_one * moment + (1.0 - beta_one) * gradient
    second_new = beta_two * second + (1.0 - beta_two) * gradient * gradient
    correct_one = 1.0 - beta_one**step_count
    correct_two = 1.0 - beta_two**step_count
    policy_new = policy - learn_rate * (moment_new / correct_one) / (
        jnp.sqrt(second_new / correct_two) + adam_epsilon
    )
    anchor_new = blend_rate * policy_new + (1.0 - blend_rate) * anchor
    return (policy_new, anchor_new, moment_new, second_new)


def token_scores(values, readout):
    return jnp.sum(jax.nn.log_sigmoid(values * readout[None, :]), axis=1)


def sequence_margin(policy_values, anchor_values, readout, sequence_length):
    token_gap = token_scores(policy_values, readout) - token_scores(anchor_values, readout)
    return jnp.mean(token_gap.reshape(-1, sequence_length), axis=1)


def pair_losses(margins, pair_index, noisy_flags):
    sequence_index = jnp.arange(margins.shape[0], dtype=jnp.int32)
    chosen = jnp.sum(
        jnp.where(pair_index[:, 0:1] == sequence_index[None, :], margins[None, :], 0.0), axis=1
    )
    rejected = jnp.sum(
        jnp.where(pair_index[:, 1:2] == sequence_index[None, :], margins[None, :], 0.0), axis=1
    )
    margin_gap = chosen - rejected
    logit_value = jnp.where(noisy_flags == 1, -margin_gap, margin_gap)
    return -(1.0 - smoothing) * jax.nn.log_sigmoid(logit_value) - smoothing * jax.nn.log_sigmoid(
        -logit_value
    )


def shards(tokens, cotangent, policy, anchor, moment, second, readout, pair_index, noisy_flags):
    part_sum = lax.psum_scatter(
        lax.dot_general(
            tokens, cotangent, (((0,), (0,)), ((), ())), preferred_element_type=jnp.float32
        ),
        "fsdp",
        scatter_dimension=0,
        tiled=True,
    )
    gradient = lax.psum(part_sum.astype(jnp.bfloat16), "rep").astype(jnp.float32)
    policy_next, anchor_next, moment_next, second_next = adam_update(
        gradient, policy, anchor, moment, second
    )
    policy_half = policy_next.astype(jnp.bfloat16)
    anchor_half = anchor_next.astype(jnp.bfloat16)
    policy_whole = lax.all_gather(policy_half, "fsdp", axis=0, tiled=True)
    anchor_whole = lax.all_gather(anchor_half, "fsdp", axis=0, tiled=True)
    policy_values = jnp.dot(tokens, policy_whole, preferred_element_type=jnp.float32)
    anchor_values = jnp.dot(tokens, anchor_whole, preferred_element_type=jnp.float32)
    margins_own = sequence_margin(policy_values, anchor_values, readout, LEN)
    all_margins = lax.all_gather(margins_own, ("rep", "fsdp"), axis=0, tiled=True)
    pair_loss = pair_losses(all_margins, pair_index, noisy_flags)
    return (policy_next, anchor_next, moment_next, second_next, pair_loss)


LOG2E = 1.4426950408889634
PLANES = 4
MESH_ID = pl.DeviceIdType.MESH


def policy_update(gradient, policy, moment, second):
    moment_new = beta_one * moment + (1.0 - beta_one) * gradient
    second_new = beta_two * second + (1.0 - beta_two) * gradient * gradient
    correct_one = 1.0 - beta_one**step_count
    correct_two = 1.0 - beta_two**step_count
    return policy - learn_rate * (moment_new / correct_one) / (
        jnp.sqrt(second_new / correct_two) + adam_epsilon
    )


def fused_kernel(
    sizes,
    tokens,
    cotangent,
    policy,
    anchor,
    moment,
    second,
    readout,
    pair_index,
    noisy_flags,
    gradient_out,
    loss_out,
    tok,
    cot,
    cot_t,
    anc,
    anc_send,
    par,
    send_a1,
    recv_a1,
    keep_a,
    send_b1,
    recv_b1,
    keep_b,
    send_a2,
    recv_a2,
    send_b2,
    recv_b2,
    send_z,
    recv_z,
    grad_own,
    result,
    weights,
    acc,
    table,
    own_sem,
    tok_sem,
    anc_sem,
    rs_recv,
    xy_recv,
    z_recv,
    out_sem,
    sent_sem,
):
    n, rows, tokens_own, half = sizes
    block = 2 * rows
    span = 4 * block
    pair = 2 * block
    low = half // 2
    me = lax.axis_index("fsdp")
    core = me % 2
    px = (me // 2) % 2
    py = (me // 4) % 2
    pz = me // 8
    chip = me // 2
    mate = me + 1 - 2 * core
    x_mate = me + 2 - 4 * px
    y_mate = me + 4 - 8 * py
    home = chip * block

    top = pz // 2
    near = pz + top * (3 - 2 * pz)
    middle = jnp.logical_and(pz > 0, pz < PLANES - 1)

    def plane(t):
        there = (near, 1 - near, 2, 3)[t]
        return there + top * (3 - 2 * there)

    def z_mate(t):
        return me + 8 * (plane(t) - pz)

    def remote(src, dst, send_sem, recv_sem, device):
        return pltpu.make_async_remote_copy(
            src_ref=src,
            dst_ref=dst,
            send_sem=send_sem,
            recv_sem=recv_sem,
            device_id={"fsdp": device},
            device_id_type=MESH_ID,
        )

    def await_bytes(ref, sem):
        pltpu.make_async_copy(ref, ref, sem).wait()

    barrier = pltpu.get_barrier_semaphore()
    others = [mate, x_mate, y_mate] + [z_mate(t) for t in (1, 2, 3)]
    for other in others:
        pl.semaphore_signal(barrier, inc=1, device_id={"fsdp": other}, device_id_type=MESH_ID)

    mine = pl.ds(pl.multiple_of(core * half, half), half)
    theirs = pl.ds(pl.multiple_of((1 - core) * half, half), half)
    params = (policy, moment, second)

    def columns(i, dy):
        start = plane(3 - i) * span + ((py + dy) % 2) * pair
        return pl.ds(pl.multiple_of(start, pair), pair)

    pieces = [(i, dy) for i in range(PLANES) for dy in (1, 0)]

    for r, side in enumerate((mine, theirs)):
        pltpu.make_async_copy(anchor.at[:, side], anc.at[r], anc_sem.at[r]).start()
    pltpu.make_async_copy(cotangent.at[:, mine], cot.at[core], own_sem.at[0]).start()

    def load(j):
        where = columns(*pieces[j])
        pltpu.make_async_copy(
            tokens.at[:, where], tok.at[core, :, where], tok_sem.at[j]
        ).start()

    load(0)
    load(1)
    pl.semaphore_wait(barrier, len(others))

    unit = half * 2
    sent = {}

    def launch(group, src, dst, recv_sem, device):
        remote(src, dst, sent_sem.at[group], recv_sem, device).start()
        count = 1
        for extent in src.shape:
            count *= extent
        sent[group] = sent.get(group, 0) + count * jnp.dtype(src.dtype).itemsize // unit

    SWAP, REDUCE, SPREAD, POLICY, CHAIN, MARGIN, TOKENS = range(7)

    launch(SWAP, cotangent.at[:, theirs], cot.at[core], own_sem.at[0], mate)
    own_rows = pl.ds(pl.multiple_of(home + core * rows, rows), rows)
    await_bytes(anc.at[1], anc_sem.at[1])
    anc_send[...] = anc[1].astype(jnp.bfloat16)
    launch(SWAP, anc_send, weights.at[1, own_rows, :], anc_sem.at[2], mate)
    await_bytes(anc.at[0], anc_sem.at[0])
    weights[1, own_rows, :] = anc[0].astype(jnp.bfloat16)

    def chip_at(zz, dy, dx):
        return zz * 4 + ((py + dy) % 2) * 2 + (px + dx) % 2

    kinds = {
        "a": (1, 0, block),
        "p": (0, 0, block),
    }

    def part(kind, k, which=None):
        m, start, count = kinds[kind]
        if which is not None:
            count = count // 2
            start = start + which * count
        return weights.at[m, pl.ds(pl.multiple_of(k * block + start, 16), count), :]

    def some_rows(count, m=0):
        return weights.at[m, pl.ds(0, count), :]

    def spread(kind, q, zz):
        ref = part(kind, chip_at(zz, 0, 0))
        group = POLICY if kind == "p" else SPREAD
        launch(group, ref, ref, xy_recv.at[q, 0], x_mate)
        launch(group, ref, ref, xy_recv.at[q, 0], y_mate)

    def relay(kind, q, zz):
        await_bytes(some_rows(2 * kinds[kind][2]), xy_recv.at[q, 0])
        forward(kind, q, zz)

    def forward(kind, q, zz):
        group = POLICY if kind == "p" else SPREAD
        ref = part(kind, chip_at(zz, 1, 0), 0)
        launch(group, ref, ref, xy_recv.at[q, 1], x_mate)
        ref = part(kind, chip_at(zz, 0, 1), 1)
        launch(group, ref, ref, xy_recv.at[q, 1], y_mate)

    def relayed(kind, q):
        await_bytes(some_rows(kinds[kind][2]), xy_recv.at[q, 1])

    def z_out(kind, q, k):
        for t in (1, 2, 3):
            ref = part(kind, k)
            launch(SPREAD, ref, ref, z_recv.at[q, pz], z_mate(t))

    def beside(kind, q, dy, dx):
        ref = part(kind, chip_at(pz, dy, dx))
        group = POLICY if kind == "p" else SPREAD
        launch(group, ref, ref, z_recv.at[q, 0], z_mate(1))

    def z_in(q, t, count):
        await_bytes(some_rows(count), z_recv.at[q, plane(t)])

    def chain_each(t, act):
        zz = plane(t)
        ref = part("p", chip_at(zz, 0, 0))

        def to(device):
            act(remote(ref, ref, sent_sem.at[CHAIN], z_recv.at[2, zz], device))

        if t < PLANES - 1:
            pl.when(jnp.logical_and(zz <= pz, pz < PLANES - 1))(lambda: to((me + 8) % n))
            pl.when(jnp.logical_and(zz >= pz, pz > 0))(lambda: to((me + n - 8) % n))
        if t == 0:
            pl.when(jnp.logical_not(middle))(lambda: to(z_mate(3)))

    def chain_step(t):
        if t > 0:
            z_in(2, t, block)
        chain_each(t, lambda copy: copy.start())

    for j in range(2, len(pieces)):
        load(j)
    for j, key in enumerate(pieces):
        where = columns(*key)
        launch(TOKENS, tokens.at[:, where], tok.at[core, :, where], tok_sem.at[j], mate)
    for a in range(3):
        pltpu.make_async_copy(params[a].at[:, mine], par.at[a, core], own_sem.at[1]).start()
        launch(SWAP, params[a].at[:, theirs], par.at[a, core], own_sem.at[1], mate)

    await_bytes(anc_send, anc_sem.at[2])
    z_out("a", 1, chip)
    spread("a", 0, pz)

    await_bytes(cot, own_sem.at[0])
    for r in range(2):
        cot_t[:, r * tokens_own : (r + 1) * tokens_own] = (
            cot[r].astype(jnp.float32).T.astype(jnp.bfloat16)
        )

    def first(key):
        await_bytes(tok.at[:, :, columns(*key)], tok_sem.at[pieces.index(key)])

    def block_gradient(i, dy, dx):
        target = chip_at(plane(3 - i), dy, dx)
        where = pl.ds(pl.multiple_of(target * block, block), block)
        total = jnp.dot(
            cot_t[:, :tokens_own], tok[0, :, where], preferred_element_type=jnp.float32
        )
        total += jnp.dot(
            cot_t[:, tokens_own:], tok[1, :, where], preferred_element_type=jnp.float32
        )
        if dx == 1:
            send_a1[i, dy] = total[:low].astype(jnp.bfloat16)
        else:
            keep_a[i, dy] = total[:low]
        if dy == 1:
            send_b1[i, dx] = total[low:].astype(jnp.bfloat16)
        else:
            keep_b[i, dx] = total[low:]

    def send_b(*at):
        launch(REDUCE, send_b1.at[at], recv_b1.at[at], rs_recv.at[1, at[0]], y_mate)

    def send_a(*at):
        launch(REDUCE, send_a1.at[at], recv_a1.at[at], rs_recv.at[0, at[0]], x_mate)

    def stage_one(i, hold=False):
        first((i, 1))
        block_gradient(i, 1, 1)
        if not hold:
            send_a(i, 1)
            send_b(i, 1)
        block_gradient(i, 1, 0)
        if not hold:
            send_b(i, 0)
        first((i, 0))
        block_gradient(i, 0, 1)
        if not hold:
            send_a(i, 0)
        block_gradient(i, 0, 0)

    def stage_two(i):
        await_bytes(recv_a1.at[i], rs_recv.at[0, i])
        send_a2[i] = (keep_a[i, 1] + recv_a1[i, 1].astype(jnp.float32)).astype(jnp.bfloat16)
        launch(REDUCE, send_a2.at[i], recv_a2.at[i], rs_recv.at[2, i], y_mate)
        await_bytes(recv_b1.at[i], rs_recv.at[1, i])
        send_b2[i] = (keep_b[i, 1] + recv_b1[i, 1].astype(jnp.float32)).astype(jnp.bfloat16)
        launch(REDUCE, send_b2.at[i], recv_b2.at[i], rs_recv.at[3, i], x_mate)

    def stage_three(i):
        await_bytes(recv_a2.at[i], rs_recv.at[2, i])
        total_a = keep_a[i, 0] + recv_a1[i, 0].astype(jnp.float32) + recv_a2[i].astype(jnp.float32)
        await_bytes(recv_b2.at[i], rs_recv.at[3, i])
        total_b = keep_b[i, 0] + recv_b1[i, 0].astype(jnp.float32) + recv_b2[i].astype(jnp.float32)
        if i == PLANES - 1:
            grad_own[:low] = total_a
            grad_own[low:] = total_b
        else:
            send_z[i, :low] = total_a.astype(jnp.bfloat16)
            send_z[i, low:] = total_b.astype(jnp.bfloat16)
            launch(REDUCE, send_z.at[i], recv_z.at[pz], rs_recv.at[4, 0], z_mate(3 - i))

    def anchor_spread(t):
        z_in(1, t, block)
        spread("a", t, plane(t))

    def anchor_relay(t):
        relay("a", t, plane(t))

    stage_one(0)
    stage_one(1)
    stage_one(2, hold=True)
    stage_two(0)
    send_b(2)
    send_a(2)
    await_bytes(some_rows(2 * block, 1), xy_recv.at[0, 0])
    beside("a", 0, 0, 1)
    stage_one(3, hold=True)
    stage_two(1)
    stage_three(0)
    beside("a", 0, 1, 0)
    forward("a", 0, pz)
    stage_two(2)
    send_b(3)
    send_a(3)
    stage_three(1)
    anchor_spread(2)
    stage_three(2)
    relayed("a", 0)
    beside("a", 0, 1, 1)
    stage_two(3)
    anchor_relay(2)
    await_bytes(par, own_sem.at[1])
    await_bytes(recv_z.at[pl.ds(0, PLANES - 1)], rs_recv.at[4, 0])
    stage_three(3)
    gradient = grad_own[...]
    for t in (1, 2, 3):
        gradient += recv_z[plane(t)].astype(jnp.float32)
    gradient = gradient.T
    for r in range(2):
        own = gradient[r * rows : (r + 1) * rows]
        updated = policy_update(own, par[0, r], par[1, r], par[2, r])
        result[r] = own
        weights[0, pl.ds(pl.multiple_of(home + r * rows, rows), rows), :] = updated.astype(
            jnp.bfloat16
        )
    chain_step(0)
    spread("p", 4, pz)

    tile = tokens_own
    scale = readout[core] * LOG2E
    blend_scale = scale * blend_rate
    anchor_scale = scale * (1.0 - blend_rate)

    def score_sum(values):
        low_part = jnp.minimum(values, 0.0).reshape(LEN // 8, 8, half)
        factor = (1.0 + jnp.exp2(-jnp.abs(values))).reshape(LEN // 8, 8, half)
        product = factor[0]
        for j in range(1, LEN // 8):
            product = product * factor[j]
        return jnp.sum(low_part, axis=0) - jnp.log2(product)

    def multiply(m, zz, t):
        where = pl.ds(pl.multiple_of(zz * span, span), span)

        @pl.loop(0, 2)
        def _(i):
            value = jnp.dot(
                tok[i, :, where], weights[m, where, :], preferred_element_type=jnp.float32
            )
            value = value if t == 0 else acc[m, i] + value
            acc[m, i] = value * anchor_scale if m == 1 and t == PLANES - 1 else value

    def anchor_multiply(t):
        if t == 1:
            z_in(1, 1, block)
            await_bytes(some_rows(3 * block), z_recv.at[0, 0])
        elif t > 1:
            relayed("a", t)
        multiply(1, plane(t), t)

    first_plane = jnp.where(middle, plane(2), plane(3))
    last_plane = jnp.where(middle, plane(3), plane(2))

    def spot(zz, dy, dx):
        return pl.ds(pl.multiple_of(chip_at(zz, dy, dx) * block, block), block)

    def compute_near(zz):
        @pl.loop(0, 2)
        def _(i):
            value = acc[0, i]
            for dy, dx in ((0, 0), (0, 1), (1, 0)):
                where = spot(zz, dy, dx)
                value += jnp.dot(
                    tok[i, :, where], weights[0, where, :], preferred_element_type=jnp.float32
                )
            acc[0, i] = value

    def compute_last(zz):
        where = spot(zz, 1, 1)

        @pl.loop(0, 2)
        def _(i):
            value = acc[0, i] + jnp.dot(
                tok[i, :, where], weights[0, where, :], preferred_element_type=jnp.float32
            )
            acc[1, i] = value * blend_scale + acc[1, i]
            acc[0, i] = value * scale
            for j in range(tile // LEN):
                gap = score_sum(acc[0, i, j * LEN : (j + 1) * LEN]) - score_sum(
                    acc[1, i, j * LEN : (j + 1) * LEN]
                )
                gap = jnp.sum(gap, axis=0, keepdims=True)
                gap = jnp.sum(gap, axis=1, keepdims=True)
                table[me, pl.ds(i * (tile // LEN) + j, 1), :] = jnp.broadcast_to(
                    gap * (1.0 / (LEN * LOG2E)), (1, 128)
                )

    pltpu.make_async_copy(result.at[core], gradient_out.at[:, mine], out_sem.at[0]).start()
    launch(REDUCE, result.at[1 - core], gradient_out.at[:, mine], out_sem.at[0], mate)

    anchor_spread(3)
    anchor_multiply(0)
    relay("p", 4, pz)

    @pl.when(middle)
    def _():
        chain_step(1)
        chain_step(2)

    beside("p", 3, 0, 1)
    beside("p", 3, 1, 0)
    anchor_multiply(2)
    anchor_relay(3)
    pl.when(jnp.logical_not(middle))(lambda: chain_step(3))
    spread("p", 5, first_plane)
    relayed("p", 4)
    beside("p", 3, 1, 1)
    multiply(0, pz, 0)

    @pl.when(middle)
    def _():
        chain_step(3)

    @pl.when(jnp.logical_not(middle))
    def _():
        chain_step(2)

    spread("p", 6, last_plane)
    anchor_multiply(1)
    relay("p", 5, first_plane)
    anchor_multiply(3)
    relay("p", 6, last_plane)
    relayed("p", 5)
    multiply(0, first_plane, 2)
    pl.when(jnp.logical_not(middle))(lambda: chain_step(1))
    await_bytes(some_rows(3 * block), z_recv.at[3, 0])
    multiply(0, plane(1), 1)
    compute_near(last_plane)
    await_bytes(gradient_out, out_sem.at[0])
    await_bytes(tok.at[0], sent_sem.at[TOKENS])
    for group in (SWAP, REDUCE, SPREAD, POLICY):
        await_bytes(some_rows(sent[group]), sent_sem.at[group])
    pl.when(middle)(lambda: await_bytes(some_rows(4 * block), sent_sem.at[CHAIN]))
    pl.when(jnp.logical_not(middle))(lambda: await_bytes(some_rows(2 * block), sent_sem.at[CHAIN]))
    relayed("p", 6)
    compute_last(last_plane)

    everyone = [
        (t, dy, dx, dc) for t in (3, 2, 1, 0) for dy, dx, dc in itertools.product((1, 0), repeat=3)
    ][:-1]
    for t, dy, dx, dc in everyone:
        there = chip_at(plane(t), dy, dx) * 2 + (core + dc) % 2
        ref = table.at[me]
        remote(ref, ref, sent_sem.at[MARGIN], out_sem.at[1], there).start()
    await_bytes(table.at[pl.ds(0, n - 1)], out_sem.at[1])
    await_bytes(table.at[pl.ds(0, n - 1)], sent_sem.at[MARGIN])
    margins = table[...].reshape(n // 2, 2, -1, 128)
    margins = (margins[:, 0] + margins[:, 1]).reshape(-1, 128)
    sequence = lax.broadcasted_iota(jnp.int32, margins.shape, 0)

    def margin_of(index):
        return jnp.sum(jnp.where(sequence == index, margins, 0.0), axis=0, keepdims=True)

    for p in range(noisy_flags.shape[0]):
        gap = margin_of(pair_index[p, 0]) - margin_of(pair_index[p, 1])
        gap = jnp.where(noisy_flags[p] == 1, -gap, gap)
        tail = jnp.log(1.0 + jnp.exp(-jnp.abs(gap)))
        loss = (1.0 - smoothing) * (tail - jnp.minimum(gap, 0.0)) + smoothing * (
            tail + jnp.maximum(gap, 0.0)
        )
        loss_out[p] = loss[0, 0]


def finish_kernel(
    gradient,
    policy,
    anchor,
    moment,
    second,
    loss,
    policy_out,
    anchor_out,
    moment_out,
    second_out,
    loss_out,
):
    updated = adam_update(gradient[...], policy[...], anchor[...], moment[...], second[...])
    for out, value in zip((policy_out, anchor_out, moment_out, second_out), updated):
        out[...] = value
    for p in range(loss.shape[0]):
        loss_out[p] = loss[p]


def fused_shards(n, tokens, cotangent, policy, anchor, moment, second, readout, pair_index, noisy_flags):
    tokens_own, depth = tokens.shape
    rows, channels = policy.shape
    half = channels // 2
    block = 2 * rows
    low = half // 2
    sizes = (n, rows, tokens_own, half)
    bf, f32 = jnp.bfloat16, jnp.float32
    vmem, dma = pltpu.VMEM, pltpu.SemaphoreType.DMA
    hbm = pl.BlockSpec(memory_space=pl.ANY)
    whole = pl.BlockSpec(memory_space=pltpu.VMEM)
    smem = pl.BlockSpec(memory_space=pltpu.SMEM)
    weight = jax.ShapeDtypeStruct((rows, channels), f32)
    losses = jax.ShapeDtypeStruct(noisy_flags.shape, f32)
    gradient, loss = pl.pallas_call(
        functools.partial(fused_kernel, sizes),
        out_shape=(pltpu.VMEM((rows, channels), f32), losses),
        in_specs=[hbm] * 6 + [whole] + [smem] * 2,
        out_specs=(hbm, smem),
        scratch_shapes=[
            vmem((2, tokens_own, depth), bf),
            vmem((2, tokens_own, half), bf),
            vmem((half, 2 * tokens_own), bf),
            vmem((2, rows, half), f32),
            vmem((rows, half), bf),
            vmem((3, 2, rows, half), f32),
            vmem((4, 2, low, block), bf),
            vmem((4, 2, low, block), bf),
            vmem((4, 2, low, block), f32),
            vmem((4, 2, low, block), bf),
            vmem((4, 2, low, block), bf),
            vmem((4, 2, low, block), f32),
            vmem((4, low, block), bf),
            vmem((4, low, block), bf),
            vmem((4, low, block), bf),
            vmem((4, low, block), bf),
            vmem((3, half, block), bf),
            vmem((4, half, block), bf),
            vmem((half, block), f32),
            vmem((2, rows, half), f32),
            vmem((2, depth, half), bf),
            vmem((2, 2, tokens_own, half), f32),
            vmem((n, 2 * tokens_own // LEN, 128), f32),
            dma((2,)),
            dma((8,)),
            dma((3,)),
            dma((5, 4)),
            dma((7, 2)),
            dma((4, 4)),
            dma((2,)),
            dma((7,)),
        ],
        compiler_params=pltpu.CompilerParams(
            collective_id=0, has_side_effects=True, vmem_limit_bytes=56 * 1024 * 1024
        ),
    )(
        tokens,
        cotangent,
        policy,
        anchor,
        moment,
        second,
        readout.reshape(2, 1, half),
        pair_index,
        noisy_flags,
    )
    policy_next, anchor_next, moment_next, second_next, pair_loss = pl.pallas_call(
        finish_kernel,
        out_shape=(weight,) * 4 + (losses,),
        in_specs=[whole] * 5 + [smem],
        out_specs=(whole,) * 4 + (smem,),
    )(*(pltpu.with_memory_space_constraint(x, pltpu.VMEM) for x in (gradient, policy, anchor, moment, second)), loss)
    return (policy_next, anchor_next, moment_next, second_next, pair_loss)


def solution(mesh):
    placed = (
        P(("rep", "fsdp"), None),
        P(("rep", "fsdp"), None),
        P("fsdp", None),
        P("fsdp", None),
        P("fsdp", None),
        P("fsdp", None),
        P(),
        P(("rep", "fsdp"), None),
        P(("rep", "fsdp")),
    )
    n = mesh.shape["fsdp"]
    body = shards
    if mesh.shape["rep"] == 1 and n == 8 * PLANES:
        body = functools.partial(fused_shards, n)
    return jax.shard_map(
        body,
        mesh=mesh,
        in_specs=placed,
        out_specs=(
            P("fsdp", None),
            P("fsdp", None),
            P("fsdp", None),
            P("fsdp", None),
            P(("rep", "fsdp")),
        ),
        check_vma=False,
    )
```

```python
import functools
import itertools
import jax
import jax.numpy as jnp
from jax import lax
from jax.experimental import pallas as pl
from jax.experimental.pallas import tpu as pltpu
from jax.sharding import PartitionSpec as P

LEN = 192


beta_one = 0.9
beta_two = 0.95
step_count = 20
learn_rate = 0.003
adam_epsilon = 1e-08
blend_rate = 0.6
smoothing = 0.1


def adam_update(gradient, policy, anchor, moment, second):
    moment_new = beta_one * moment + (1.0 - beta_one) * gradient
    second_new = beta_two * second + (1.0 - beta_two) * gradient * gradient
    correct_one = 1.0 - beta_one**step_count
    correct_two = 1.0 - beta_two**step_count
    policy_new = policy - learn_rate * (moment_new / correct_one) / (
        jnp.sqrt(second_new / correct_two) + adam_epsilon
    )
    anchor_new = blend_rate * policy_new + (1.0 - blend_rate) * anchor
    return (policy_new, anchor_new, moment_new, second_new)


def token_scores(values, readout):
    return jnp.sum(jax.nn.log_sigmoid(values * readout[None, :]), axis=1)


def sequence_margin(policy_values, anchor_values, readout, sequence_length):
    token_gap = token_scores(policy_values, readout) - token_scores(anchor_values, readout)
    return jnp.mean(token_gap.reshape(-1, sequence_length), axis=1)


def pair_losses(margins, pair_index, noisy_flags):
    sequence_index = jnp.arange(margins.shape[0], dtype=jnp.int32)
    chosen = jnp.sum(
        jnp.where(pair_index[:, 0:1] == sequence_index[None, :], margins[None, :], 0.0), axis=1
    )
    rejected = jnp.sum(
        jnp.where(pair_index[:, 1:2] == sequence_index[None, :], margins[None, :], 0.0), axis=1
    )
    margin_gap = chosen - rejected
    logit_value = jnp.where(noisy_flags == 1, -margin_gap, margin_gap)
    return -(1.0 - smoothing) * jax.nn.log_sigmoid(logit_value) - smoothing * jax.nn.log_sigmoid(
        -logit_value
    )


def shards(tokens, cotangent, policy, anchor, moment, second, readout, pair_index, noisy_flags):
    part_sum = lax.psum_scatter(
        lax.dot_general(
            tokens, cotangent, (((0,), (0,)), ((), ())), preferred_element_type=jnp.float32
        ),
        "fsdp",
        scatter_dimension=0,
        tiled=True,
    )
    gradient = lax.psum(part_sum.astype(jnp.bfloat16), "rep").astype(jnp.float32)
    policy_next, anchor_next, moment_next, second_next = adam_update(
        gradient, policy, anchor, moment, second
    )
    policy_half = policy_next.astype(jnp.bfloat16)
    anchor_half = anchor_next.astype(jnp.bfloat16)
    policy_whole = lax.all_gather(policy_half, "fsdp", axis=0, tiled=True)
    anchor_whole = lax.all_gather(anchor_half, "fsdp", axis=0, tiled=True)
    policy_values = jnp.dot(tokens, policy_whole, preferred_element_type=jnp.float32)
    anchor_values = jnp.dot(tokens, anchor_whole, preferred_element_type=jnp.float32)
    margins_own = sequence_margin(policy_values, anchor_values, readout, LEN)
    all_margins = lax.all_gather(margins_own, ("rep", "fsdp"), axis=0, tiled=True)
    pair_loss = pair_losses(all_margins, pair_index, noisy_flags)
    return (policy_next, anchor_next, moment_next, second_next, pair_loss)


LOG2E = 1.4426950408889634
PLANES = 4
MESH_ID = pl.DeviceIdType.MESH


def policy_update(gradient, policy, moment, second):
    moment_new = beta_one * moment + (1.0 - beta_one) * gradient
    second_new = beta_two * second + (1.0 - beta_two) * gradient * gradient
    correct_one = 1.0 - beta_one**step_count
    correct_two = 1.0 - beta_two**step_count
    return policy - learn_rate * (moment_new / correct_one) / (
        jnp.sqrt(second_new / correct_two) + adam_epsilon
    )


def fused_kernel(
    sizes,
    tokens,
    cotangent,
    policy,
    anchor,
    moment,
    second,
    readout,
    pair_index,
    noisy_flags,
    gradient_out,
    loss_out,
    tok,
    cot,
    cot_t,
    anc,
    anc_send,
    par,
    send_a1,
    recv_a1,
    keep_a,
    send_b1,
    recv_b1,
    keep_b,
    send_a2,
    recv_a2,
    send_b2,
    recv_b2,
    send_z,
    recv_z,
    grad_own,
    result,
    weights,
    acc,
    table,
    own_sem,
    tok_sem,
    anc_sem,
    rs_recv,
    xy_recv,
    z_recv,
    out_sem,
    sent_sem,
):
    n, rows, tokens_own, half = sizes
    block = 2 * rows
    span = 4 * block
    pair = 2 * block
    low = half // 2
    me = lax.axis_index("fsdp")
    core = me % 2
    px = (me // 2) % 2
    py = (me // 4) % 2
    pz = me // 8
    chip = me // 2
    mate = me + 1 - 2 * core
    x_mate = me + 2 - 4 * px
    y_mate = me + 4 - 8 * py
    home = chip * block

    top = pz // 2
    near = pz + top * (3 - 2 * pz)
    middle = jnp.logical_and(pz > 0, pz < PLANES - 1)

    def plane(t):
        there = (near, 1 - near, 2, 3)[t]
        return there + top * (3 - 2 * there)

    def z_mate(t):
        return me + 8 * (plane(t) - pz)

    def remote(src, dst, send_sem, recv_sem, device):
        return pltpu.make_async_remote_copy(
            src_ref=src,
            dst_ref=dst,
            send_sem=send_sem,
            recv_sem=recv_sem,
            device_id={"fsdp": device},
            device_id_type=MESH_ID,
        )

    def await_bytes(ref, sem):
        pltpu.make_async_copy(ref, ref, sem).wait()

    barrier = pltpu.get_barrier_semaphore()
    others = [mate, x_mate, y_mate] + [z_mate(t) for t in (1, 2, 3)]
    for other in others:
        pl.semaphore_signal(barrier, inc=1, device_id={"fsdp": other}, device_id_type=MESH_ID)

    mine = pl.ds(pl.multiple_of(core * half, half), half)
    theirs = pl.ds(pl.multiple_of((1 - core) * half, half), half)
    params = (policy, moment, second)

    def columns(i, dy):
        start = plane(3 - i) * span + ((py + dy) % 2) * pair
        return pl.ds(pl.multiple_of(start, pair), pair)

    pieces = [(i, dy) for i in range(PLANES) for dy in (1, 0)]

    for r, side in enumerate((mine, theirs)):
        pltpu.make_async_copy(anchor.at[:, side], anc.at[r], anc_sem.at[r]).start()
    pltpu.make_async_copy(cotangent.at[:, mine], cot.at[core], own_sem.at[0]).start()

    def load(j):
        where = columns(*pieces[j])
        pltpu.make_async_copy(
            tokens.at[:, where], tok.at[core, :, where], tok_sem.at[j]
        ).start()

    load(0)
    load(1)
    pl.semaphore_wait(barrier, len(others))

    unit = half * 2
    sent = {}

    def launch(group, src, dst, recv_sem, device):
        remote(src, dst, sent_sem.at[group], recv_sem, device).start()
        count = 1
        for extent in src.shape:
            count *= extent
        sent[group] = sent.get(group, 0) + count * jnp.dtype(src.dtype).itemsize // unit

    SWAP, REDUCE, SPREAD, POLICY, CHAIN, MARGIN, TOKENS = range(7)

    launch(SWAP, cotangent.at[:, theirs], cot.at[core], own_sem.at[0], mate)
    own_rows = pl.ds(pl.multiple_of(home + core * rows, rows), rows)
    await_bytes(anc.at[1], anc_sem.at[1])
    anc_send[...] = anc[1].astype(jnp.bfloat16)
    launch(SWAP, anc_send, weights.at[1, own_rows, :], anc_sem.at[2], mate)
    await_bytes(anc.at[0], anc_sem.at[0])
    weights[1, own_rows, :] = anc[0].astype(jnp.bfloat16)

    def chip_at(zz, dy, dx):
        return zz * 4 + ((py + dy) % 2) * 2 + (px + dx) % 2

    kinds = {
        "a": (1, 0, block),
        "p": (0, 0, block),
        "u": (0, 0, rows),
        "v": (0, rows, rows),
    }

    def part(kind, k, which=None):
        m, start, count = kinds[kind]
        if which is not None:
            count = count // 2
            start = start + which * count
        return weights.at[m, pl.ds(pl.multiple_of(k * block + start, 16), count), :]

    def some_rows(count, m=0):
        return weights.at[m, pl.ds(0, count), :]

    def spread(kind, q, zz):
        ref = part(kind, chip_at(zz, 0, 0))
        group = SPREAD if kind == "a" else POLICY
        launch(group, ref, ref, xy_recv.at[q, 0], x_mate)
        launch(group, ref, ref, xy_recv.at[q, 0], y_mate)

    def relay(kind, q, zz):
        await_bytes(some_rows(2 * kinds[kind][2]), xy_recv.at[q, 0])
        forward(kind, q, zz)

    def forward(kind, q, zz):
        group = SPREAD if kind == "a" else POLICY
        ref = part(kind, chip_at(zz, 1, 0), 0)
        launch(group, ref, ref, xy_recv.at[q, 1], x_mate)
        ref = part(kind, chip_at(zz, 0, 1), 1)
        launch(group, ref, ref, xy_recv.at[q, 1], y_mate)

    def relayed(kind, q):
        await_bytes(some_rows(kinds[kind][2]), xy_recv.at[q, 1])

    def z_out(kind, q, k):
        for t in (1, 2, 3):
            ref = part(kind, k)
            launch(SPREAD, ref, ref, z_recv.at[q, pz], z_mate(t))

    def beside(kind, q, dy, dx):
        ref = part(kind, chip_at(pz, dy, dx))
        group = SPREAD if kind == "a" else POLICY
        launch(group, ref, ref, z_recv.at[q, 0], z_mate(1))

    def z_in(q, t, count):
        await_bytes(some_rows(count), z_recv.at[q, plane(t)])

    def chain_start(kind, q, t):
        zz = plane(t)
        ref = part(kind, chip_at(zz, 0, 0))

        def to(device):
            remote(ref, ref, sent_sem.at[CHAIN], z_recv.at[q, zz], device).start()

        pl.when(jnp.logical_and(zz <= pz, pz < PLANES - 1))(lambda: to((me + 8) % n))
        pl.when(jnp.logical_and(zz >= pz, pz > 0))(lambda: to((me + n - 8) % n))

    def far_start(kind, q):
        ref = part(kind, chip)
        remote(ref, ref, sent_sem.at[CHAIN], z_recv.at[q, pz], z_mate(3)).start()

    def chain_wait(*ts):
        for t in ts:
            z_in(2, t, rows)
            z_in(4, t, rows)

    for j in range(2, len(pieces)):
        load(j)
    for j, key in enumerate(pieces):
        where = columns(*key)
        launch(TOKENS, tokens.at[:, where], tok.at[core, :, where], tok_sem.at[j], mate)
    for a in range(3):
        pltpu.make_async_copy(params[a].at[:, mine], par.at[a, core], own_sem.at[1]).start()
        launch(SWAP, params[a].at[:, theirs], par.at[a, core], own_sem.at[1], mate)

    await_bytes(anc_send, anc_sem.at[2])
    z_out("a", 1, chip)
    spread("a", 0, pz)

    await_bytes(cot, own_sem.at[0])
    for r in range(2):
        cot_t[:, r * tokens_own : (r + 1) * tokens_own] = (
            cot[r].astype(jnp.float32).T.astype(jnp.bfloat16)
        )

    def first(key):
        await_bytes(tok.at[:, :, columns(*key)], tok_sem.at[pieces.index(key)])

    def block_gradient(i, dy, dx):
        target = chip_at(plane(3 - i), dy, dx)
        where = pl.ds(pl.multiple_of(target * block, block), block)
        total = jnp.dot(
            cot_t[:, :tokens_own], tok[0, :, where], preferred_element_type=jnp.float32
        )
        total += jnp.dot(
            cot_t[:, tokens_own:], tok[1, :, where], preferred_element_type=jnp.float32
        )
        if dx == 1:
            send_a1[i, dy] = total[:low].astype(jnp.bfloat16)
        else:
            keep_a[i, dy] = total[:low]
        if dy == 1:
            send_b1[i, dx] = total[low:].astype(jnp.bfloat16)
        else:
            keep_b[i, dx] = total[low:]

    def send_b(*at):
        launch(REDUCE, send_b1.at[at], recv_b1.at[at], rs_recv.at[1, at[0]], y_mate)

    def send_a(*at):
        launch(REDUCE, send_a1.at[at], recv_a1.at[at], rs_recv.at[0, at[0]], x_mate)

    def stage_one(i, hold=False):
        first((i, 1))
        block_gradient(i, 1, 1)
        if not hold:
            send_a(i, 1)
            send_b(i, 1)
        block_gradient(i, 1, 0)
        if not hold:
            send_b(i, 0)
        first((i, 0))
        block_gradient(i, 0, 1)
        if not hold:
            send_a(i, 0)
        block_gradient(i, 0, 0)

    def stage_two(i):
        await_bytes(recv_a1.at[i], rs_recv.at[0, i])
        send_a2[i] = (keep_a[i, 1] + recv_a1[i, 1].astype(jnp.float32)).astype(jnp.bfloat16)
        launch(REDUCE, send_a2.at[i], recv_a2.at[i], rs_recv.at[2, i], y_mate)
        await_bytes(recv_b1.at[i], rs_recv.at[1, i])
        send_b2[i] = (keep_b[i, 1] + recv_b1[i, 1].astype(jnp.float32)).astype(jnp.bfloat16)
        launch(REDUCE, send_b2.at[i], recv_b2.at[i], rs_recv.at[3, i], x_mate)

    def stage_three(i):
        await_bytes(recv_a2.at[i], rs_recv.at[2, i])
        total_a = keep_a[i, 0] + recv_a1[i, 0].astype(jnp.float32) + recv_a2[i].astype(jnp.float32)
        await_bytes(recv_b2.at[i], rs_recv.at[3, i])
        total_b = keep_b[i, 0] + recv_b1[i, 0].astype(jnp.float32) + recv_b2[i].astype(jnp.float32)
        if i == PLANES - 1:
            grad_own[:low] = total_a
            grad_own[low:] = total_b
        else:
            send_z[i, :low] = total_a.astype(jnp.bfloat16)
            send_z[i, low:] = total_b.astype(jnp.bfloat16)
            launch(REDUCE, send_z.at[i], recv_z.at[pz], rs_recv.at[4, 0], z_mate(3 - i))

    def anchor_spread(t):
        z_in(1, t, block)
        spread("a", t, plane(t))

    def anchor_relay(t):
        relay("a", t, plane(t))

    stage_one(0)
    stage_one(1)
    stage_one(2, hold=True)
    stage_two(0)
    send_b(2)
    send_a(2)
    await_bytes(some_rows(2 * block, 1), xy_recv.at[0, 0])
    beside("a", 0, 0, 1)
    stage_one(3, hold=True)
    stage_two(1)
    stage_three(0)
    forward("a", 0, pz)
    stage_two(2)
    send_b(3)
    send_a(3)
    stage_three(1)
    anchor_spread(2)
    stage_three(2)
    beside("a", 0, 1, 0)
    relayed("a", 0)
    beside("a", 0, 1, 1)
    stage_two(3)
    anchor_relay(2)
    await_bytes(par, own_sem.at[1])
    await_bytes(recv_z.at[pl.ds(0, PLANES - 1)], rs_recv.at[4, 0])
    stage_three(3)
    gradient = grad_own[...]
    for t in (1, 2, 3):
        gradient += recv_z[plane(t)].astype(jnp.float32)
    gradient = gradient.T
    for r in range(2):
        own = gradient[r * rows : (r + 1) * rows]
        updated = policy_update(own, par[0, r], par[1, r], par[2, r])
        result[r] = own
        weights[0, pl.ds(pl.multiple_of(home + r * rows, rows), rows), :] = updated.astype(
            jnp.bfloat16
        )
    chain_start("u", 2, 0)
    chain_start("v", 4, 0)

    @pl.when(jnp.logical_not(middle))
    def _():
        far_start("u", 2)
        far_start("v", 4)

    spread("u", 4, pz)
    spread("v", 7, pz)

    tile = tokens_own
    scale = readout[core] * LOG2E
    blend_scale = scale * blend_rate
    anchor_scale = scale * (1.0 - blend_rate)

    def score_sum(values):
        low_part = jnp.minimum(values, 0.0).reshape(LEN // 8, 8, half)
        factor = (1.0 + jnp.exp2(-jnp.abs(values))).reshape(LEN // 8, 8, half)
        product = factor[0]
        for j in range(1, LEN // 8):
            product = product * factor[j]
        return jnp.sum(low_part, axis=0) - jnp.log2(product)

    def multiply(m, zz, t):
        where = pl.ds(pl.multiple_of(zz * span, span), span)

        @pl.loop(0, 2)
        def _(i):
            value = jnp.dot(
                tok[i, :, where], weights[m, where, :], preferred_element_type=jnp.float32
            )
            value = value if t == 0 else acc[m, i] + value
            acc[m, i] = value * anchor_scale if m == 1 and t == PLANES - 1 else value

    def anchor_multiply(t):
        if t == 1:
            z_in(1, 1, block)
            await_bytes(some_rows(3 * block), z_recv.at[0, 0])
        elif t > 1:
            relayed("a", t)
        multiply(1, plane(t), t)

    first_plane = jnp.where(middle, plane(2), plane(3))
    last_plane = jnp.where(middle, plane(3), plane(2))

    def spot(zz, dy, dx):
        return pl.ds(pl.multiple_of(chip_at(zz, dy, dx) * block, block), block)

    def compute_near(zz):
        @pl.loop(0, 2)
        def _(i):
            value = acc[0, i]
            for dy, dx in ((0, 0), (0, 1), (1, 0)):
                where = spot(zz, dy, dx)
                value += jnp.dot(
                    tok[i, :, where], weights[0, where, :], preferred_element_type=jnp.float32
                )
            acc[0, i] = value

    def compute_last(zz):
        where = spot(zz, 1, 1)

        @pl.loop(0, 2)
        def _(i):
            value = acc[0, i] + jnp.dot(
                tok[i, :, where], weights[0, where, :], preferred_element_type=jnp.float32
            )
            acc[1, i] = value * blend_scale + acc[1, i]
            acc[0, i] = value * scale
            for j in range(tile // LEN):
                gap = score_sum(acc[0, i, j * LEN : (j + 1) * LEN]) - score_sum(
                    acc[1, i, j * LEN : (j + 1) * LEN]
                )
                gap = jnp.sum(gap, axis=0, keepdims=True)
                gap = jnp.sum(gap, axis=1, keepdims=True)
                table[me, pl.ds(i * (tile // LEN) + j, 1), :] = jnp.broadcast_to(
                    gap * (1.0 / (LEN * LOG2E)), (1, 128)
                )

    pltpu.make_async_copy(result.at[core], gradient_out.at[:, mine], out_sem.at[0]).start()
    launch(REDUCE, result.at[1 - core], gradient_out.at[:, mine], out_sem.at[0], mate)

    anchor_spread(3)
    anchor_multiply(0)
    for kind, q, chain_q in (("u", 4, 2), ("v", 7, 4)):
        relay(kind, q, pz)

        @pl.when(middle)
        def _():
            for t in (1, 2):
                z_in(chain_q, t, rows)
                chain_start(kind, chain_q, t)

    beside("p", 3, 0, 1)
    beside("p", 3, 1, 0)
    anchor_multiply(2)
    anchor_relay(3)
    pl.when(jnp.logical_not(middle))(lambda: chain_wait(3))
    spread("p", 5, first_plane)
    relayed("u", 4)
    relayed("v", 7)
    beside("p", 3, 1, 1)
    multiply(0, pz, 0)

    pl.when(middle)(lambda: chain_wait(3))
    pl.when(jnp.logical_not(middle))(lambda: chain_wait(2))

    spread("p", 6, last_plane)
    anchor_multiply(1)
    relay("p", 5, first_plane)
    anchor_multiply(3)
    relay("p", 6, last_plane)
    compute_near(last_plane)
    relayed("p", 5)
    multiply(0, first_plane, 2)
    pl.when(jnp.logical_not(middle))(lambda: chain_wait(1))
    await_bytes(some_rows(3 * block), z_recv.at[3, 0])
    multiply(0, plane(1), 1)
    await_bytes(gradient_out, out_sem.at[0])
    await_bytes(tok.at[0], sent_sem.at[TOKENS])
    for group in (SWAP, REDUCE, SPREAD, POLICY):
        await_bytes(some_rows(sent[group]), sent_sem.at[group])
    pl.when(middle)(lambda: await_bytes(some_rows(4 * block), sent_sem.at[CHAIN]))
    pl.when(jnp.logical_not(middle))(lambda: await_bytes(some_rows(2 * block), sent_sem.at[CHAIN]))
    relayed("p", 6)
    compute_last(last_plane)

    everyone = [
        (t, dy, dx, dc) for t in (3, 2, 1, 0) for dy, dx, dc in itertools.product((1, 0), repeat=3)
    ][:-1]
    for t, dy, dx, dc in everyone:
        there = chip_at(plane(t), dy, dx) * 2 + (core + dc) % 2
        ref = table.at[me]
        remote(ref, ref, sent_sem.at[MARGIN], out_sem.at[1], there).start()
    await_bytes(table.at[pl.ds(0, n - 1)], out_sem.at[1])
    await_bytes(table.at[pl.ds(0, n - 1)], sent_sem.at[MARGIN])
    margins = table[...].reshape(n // 2, 2, -1, 128)
    margins = (margins[:, 0] + margins[:, 1]).reshape(-1, 128)
    sequence = lax.broadcasted_iota(jnp.int32, margins.shape, 0)

    def margin_of(index):
        return jnp.sum(jnp.where(sequence == index, margins, 0.0), axis=0, keepdims=True)

    for p in range(noisy_flags.shape[0]):
        gap = margin_of(pair_index[p, 0]) - margin_of(pair_index[p, 1])
        gap = jnp.where(noisy_flags[p] == 1, -gap, gap)
        tail = jnp.log(1.0 + jnp.exp(-jnp.abs(gap)))
        loss = (1.0 - smoothing) * (tail - jnp.minimum(gap, 0.0)) + smoothing * (
            tail + jnp.maximum(gap, 0.0)
        )
        loss_out[p] = loss[0, 0]


def finish_kernel(
    gradient,
    policy,
    anchor,
    moment,
    second,
    loss,
    policy_out,
    anchor_out,
    moment_out,
    second_out,
    loss_out,
):
    updated = adam_update(gradient[...], policy[...], anchor[...], moment[...], second[...])
    for out, value in zip((policy_out, anchor_out, moment_out, second_out), updated):
        out[...] = value
    for p in range(loss.shape[0]):
        loss_out[p] = loss[p]


def fused_shards(n, tokens, cotangent, policy, anchor, moment, second, readout, pair_index, noisy_flags):
    tokens_own, depth = tokens.shape
    rows, channels = policy.shape
    half = channels // 2
    block = 2 * rows
    low = half // 2
    sizes = (n, rows, tokens_own, half)
    bf, f32 = jnp.bfloat16, jnp.float32
    vmem, dma = pltpu.VMEM, pltpu.SemaphoreType.DMA
    hbm = pl.BlockSpec(memory_space=pl.ANY)
    whole = pl.BlockSpec(memory_space=pltpu.VMEM)
    smem = pl.BlockSpec(memory_space=pltpu.SMEM)
    weight = jax.ShapeDtypeStruct((rows, channels), f32)
    losses = jax.ShapeDtypeStruct(noisy_flags.shape, f32)
    gradient, loss = pl.pallas_call(
        functools.partial(fused_kernel, sizes),
        out_shape=(pltpu.VMEM((rows, channels), f32), losses),
        in_specs=[hbm] * 6 + [whole] + [smem] * 2,
        out_specs=(hbm, smem),
        scratch_shapes=[
            vmem((2, tokens_own, depth), bf),
            vmem((2, tokens_own, half), bf),
            vmem((half, 2 * tokens_own), bf),
            vmem((2, rows, half), f32),
            vmem((rows, half), bf),
            vmem((3, 2, rows, half), f32),
            vmem((4, 2, low, block), bf),
            vmem((4, 2, low, block), bf),
            vmem((4, 2, low, block), f32),
            vmem((4, 2, low, block), bf),
            vmem((4, 2, low, block), bf),
            vmem((4, 2, low, block), f32),
            vmem((4, low, block), bf),
            vmem((4, low, block), bf),
            vmem((4, low, block), bf),
            vmem((4, low, block), bf),
            vmem((3, half, block), bf),
            vmem((4, half, block), bf),
            vmem((half, block), f32),
            vmem((2, rows, half), f32),
            vmem((2, depth, half), bf),
            vmem((2, 2, tokens_own, half), f32),
            vmem((n, 2 * tokens_own // LEN, 128), f32),
            dma((2,)),
            dma((8,)),
            dma((3,)),
            dma((5, 4)),
            dma((8, 2)),
            dma((5, 4)),
            dma((2,)),
            dma((7,)),
        ],
        compiler_params=pltpu.CompilerParams(
            collective_id=0, has_side_effects=True, vmem_limit_bytes=56 * 1024 * 1024
        ),
    )(
        tokens,
        cotangent,
        policy,
        anchor,
        moment,
        second,
        readout.reshape(2, 1, half),
        pair_index,
        noisy_flags,
    )
    policy_next, anchor_next, moment_next, second_next, pair_loss = pl.pallas_call(
        finish_kernel,
        out_shape=(weight,) * 4 + (losses,),
        in_specs=[whole] * 5 + [smem],
        out_specs=(whole,) * 4 + (smem,),
    )(*(pltpu.with_memory_space_constraint(x, pltpu.VMEM) for x in (gradient, policy, anchor, moment, second)), loss)
    return (policy_next, anchor_next, moment_next, second_next, pair_loss)


def solution(mesh):
    placed = (
        P(("rep", "fsdp"), None),
        P(("rep", "fsdp"), None),
        P("fsdp", None),
        P("fsdp", None),
        P("fsdp", None),
        P("fsdp", None),
        P(),
        P(("rep", "fsdp"), None),
        P(("rep", "fsdp")),
    )
    n = mesh.shape["fsdp"]
    body = shards
    if mesh.shape["rep"] == 1 and n == 8 * PLANES:
        body = functools.partial(fused_shards, n)
    return jax.shard_map(
        body,
        mesh=mesh,
        in_specs=placed,
        out_specs=(
            P("fsdp", None),
            P("fsdp", None),
            P("fsdp", None),
            P("fsdp", None),
            P(("rep", "fsdp")),
        ),
        check_vma=False,
    )
```

```python
import functools
import itertools
import jax
import jax.numpy as jnp
from jax import lax
from jax.experimental import pallas as pl
from jax.experimental.pallas import tpu as pltpu
from jax.sharding import PartitionSpec as P

LEN = 192


beta_one = 0.9
beta_two = 0.95
step_count = 20
learn_rate = 0.003
adam_epsilon = 1e-08
blend_rate = 0.6
smoothing = 0.1


def adam_update(gradient, policy, anchor, moment, second):
    moment_new = beta_one * moment + (1.0 - beta_one) * gradient
    second_new = beta_two * second + (1.0 - beta_two) * gradient * gradient
    correct_one = 1.0 - beta_one**step_count
    correct_two = 1.0 - beta_two**step_count
    policy_new = policy - learn_rate * (moment_new / correct_one) / (
        jnp.sqrt(second_new / correct_two) + adam_epsilon
    )
    anchor_new = blend_rate * policy_new + (1.0 - blend_rate) * anchor
    return (policy_new, anchor_new, moment_new, second_new)


def token_scores(values, readout):
    return jnp.sum(jax.nn.log_sigmoid(values * readout[None, :]), axis=1)


def sequence_margin(policy_values, anchor_values, readout, sequence_length):
    token_gap = token_scores(policy_values, readout) - token_scores(anchor_values, readout)
    return jnp.mean(token_gap.reshape(-1, sequence_length), axis=1)


def pair_losses(margins, pair_index, noisy_flags):
    sequence_index = jnp.arange(margins.shape[0], dtype=jnp.int32)
    chosen = jnp.sum(
        jnp.where(pair_index[:, 0:1] == sequence_index[None, :], margins[None, :], 0.0), axis=1
    )
    rejected = jnp.sum(
        jnp.where(pair_index[:, 1:2] == sequence_index[None, :], margins[None, :], 0.0), axis=1
    )
    margin_gap = chosen - rejected
    logit_value = jnp.where(noisy_flags == 1, -margin_gap, margin_gap)
    return -(1.0 - smoothing) * jax.nn.log_sigmoid(logit_value) - smoothing * jax.nn.log_sigmoid(
        -logit_value
    )


def shards(tokens, cotangent, policy, anchor, moment, second, readout, pair_index, noisy_flags):
    part_sum = lax.psum_scatter(
        lax.dot_general(
            tokens, cotangent, (((0,), (0,)), ((), ())), preferred_element_type=jnp.float32
        ),
        "fsdp",
        scatter_dimension=0,
        tiled=True,
    )
    gradient = lax.psum(part_sum.astype(jnp.bfloat16), "rep").astype(jnp.float32)
    policy_next, anchor_next, moment_next, second_next = adam_update(
        gradient, policy, anchor, moment, second
    )
    policy_half = policy_next.astype(jnp.bfloat16)
    anchor_half = anchor_next.astype(jnp.bfloat16)
    policy_whole = lax.all_gather(policy_half, "fsdp", axis=0, tiled=True)
    anchor_whole = lax.all_gather(anchor_half, "fsdp", axis=0, tiled=True)
    policy_values = jnp.dot(tokens, policy_whole, preferred_element_type=jnp.float32)
    anchor_values = jnp.dot(tokens, anchor_whole, preferred_element_type=jnp.float32)
    margins_own = sequence_margin(policy_values, anchor_values, readout, LEN)
    all_margins = lax.all_gather(margins_own, ("rep", "fsdp"), axis=0, tiled=True)
    pair_loss = pair_losses(all_margins, pair_index, noisy_flags)
    return (policy_next, anchor_next, moment_next, second_next, pair_loss)


LOG2E = 1.4426950408889634
PLANES = 4
MESH_ID = pl.DeviceIdType.MESH


def policy_update(gradient, policy, moment, second):
    moment_new = beta_one * moment + (1.0 - beta_one) * gradient
    second_new = beta_two * second + (1.0 - beta_two) * gradient * gradient
    correct_one = 1.0 - beta_one**step_count
    correct_two = 1.0 - beta_two**step_count
    return policy - learn_rate * (moment_new / correct_one) / (
        jnp.sqrt(second_new / correct_two) + adam_epsilon
    )


def fused_kernel(
    sizes,
    tokens,
    cotangent,
    policy,
    anchor,
    moment,
    second,
    readout,
    pair_index,
    noisy_flags,
    gradient_out,
    loss_out,
    tok,
    cot,
    cot_t,
    anc,
    anc_send,
    par,
    send_a1,
    recv_a1,
    keep_a,
    send_b1,
    recv_b1,
    keep_b,
    send_a2,
    recv_a2,
    send_b2,
    recv_b2,
    send_z,
    recv_z,
    grad_own,
    result,
    weights,
    acc,
    table,
    own_sem,
    tok_sem,
    anc_sem,
    rs_recv,
    xy_recv,
    z_recv,
    out_sem,
    sent_sem,
):
    n, rows, tokens_own, half = sizes
    block = 2 * rows
    span = 4 * block
    pair = 2 * block
    low = half // 2
    me = lax.axis_index("fsdp")
    core = me % 2
    px = (me // 2) % 2
    py = (me // 4) % 2
    pz = me // 8
    chip = me // 2
    mate = me + 1 - 2 * core
    x_mate = me + 2 - 4 * px
    y_mate = me + 4 - 8 * py
    home = chip * block

    top = pz // 2
    near = pz + top * (3 - 2 * pz)
    middle = jnp.logical_and(pz > 0, pz < PLANES - 1)

    def plane(t):
        there = (near, 1 - near, 2, 3)[t]
        return there + top * (3 - 2 * there)

    def z_mate(t):
        return me + 8 * (plane(t) - pz)

    def remote(src, dst, send_sem, recv_sem, device):
        return pltpu.make_async_remote_copy(
            src_ref=src,
            dst_ref=dst,
            send_sem=send_sem,
            recv_sem=recv_sem,
            device_id={"fsdp": device},
            device_id_type=MESH_ID,
        )

    def await_bytes(ref, sem):
        pltpu.make_async_copy(ref, ref, sem).wait()

    barrier = pltpu.get_barrier_semaphore()
    others = [mate, x_mate, y_mate] + [z_mate(t) for t in (1, 2, 3)]
    for other in others:
        pl.semaphore_signal(barrier, inc=1, device_id={"fsdp": other}, device_id_type=MESH_ID)

    mine = pl.ds(pl.multiple_of(core * half, half), half)
    theirs = pl.ds(pl.multiple_of((1 - core) * half, half), half)
    params = (policy, moment, second)

    def columns(i, dy):
        start = plane(3 - i) * span + ((py + dy) % 2) * pair
        return pl.ds(pl.multiple_of(start, pair), pair)

    pieces = [(i, dy) for i in range(PLANES) for dy in (1, 0)]

    for r, side in enumerate((mine, theirs)):
        pltpu.make_async_copy(anchor.at[:, side], anc.at[r], anc_sem.at[r]).start()
    pltpu.make_async_copy(cotangent.at[:, mine], cot.at[core], own_sem.at[0]).start()

    def load(j):
        where = columns(*pieces[j])
        pltpu.make_async_copy(
            tokens.at[:, where], tok.at[core, :, where], tok_sem.at[j]
        ).start()

    load(0)
    load(1)
    pl.semaphore_wait(barrier, len(others))

    unit = half * 2
    sent = {}

    def launch(group, src, dst, recv_sem, device):
        remote(src, dst, sent_sem.at[group], recv_sem, device).start()
        count = 1
        for extent in src.shape:
            count *= extent
        sent[group] = sent.get(group, 0) + count * jnp.dtype(src.dtype).itemsize // unit

    SWAP, REDUCE, SPREAD, POLICY, CHAIN, MARGIN, TOKENS = range(7)

    launch(SWAP, cotangent.at[:, theirs], cot.at[core], own_sem.at[0], mate)
    own_rows = pl.ds(pl.multiple_of(home + core * rows, rows), rows)
    await_bytes(anc.at[1], anc_sem.at[1])
    anc_send[...] = anc[1].astype(jnp.bfloat16)
    launch(SWAP, anc_send, weights.at[1, own_rows, :], anc_sem.at[2], mate)
    await_bytes(anc.at[0], anc_sem.at[0])
    weights[1, own_rows, :] = anc[0].astype(jnp.bfloat16)

    def chip_at(zz, dy, dx):
        return zz * 4 + ((py + dy) % 2) * 2 + (px + dx) % 2

    kinds = {
        "a": (1, 0, block),
        "p": (0, 0, block),
        "u": (0, 0, rows),
        "v": (0, rows, rows),
    }

    def part(kind, k, which=None):
        m, start, count = kinds[kind]
        if which is not None:
            count = count // 2
            start = start + which * count
        return weights.at[m, pl.ds(pl.multiple_of(k * block + start, 16), count), :]

    def some_rows(count, m=0):
        return weights.at[m, pl.ds(0, count), :]

    def spread(kind, q, zz):
        ref = part(kind, chip_at(zz, 0, 0))
        group = SPREAD if kind == "a" else POLICY
        launch(group, ref, ref, xy_recv.at[q, 0], x_mate)
        launch(group, ref, ref, xy_recv.at[q, 0], y_mate)

    def relay(kind, q, zz):
        await_bytes(some_rows(2 * kinds[kind][2]), xy_recv.at[q, 0])
        forward(kind, q, zz)

    def forward(kind, q, zz):
        group = SPREAD if kind == "a" else POLICY
        ref = part(kind, chip_at(zz, 1, 0), 0)
        launch(group, ref, ref, xy_recv.at[q, 1], x_mate)
        ref = part(kind, chip_at(zz, 0, 1), 1)
        launch(group, ref, ref, xy_recv.at[q, 1], y_mate)

    def relayed(kind, q):
        await_bytes(some_rows(kinds[kind][2]), xy_recv.at[q, 1])

    def z_out(kind, q, k):
        for t in (1, 2, 3):
            ref = part(kind, k)
            launch(SPREAD, ref, ref, z_recv.at[q, pz], z_mate(t))

    def beside(kind, q, dy, dx, which=None):
        ref = part(kind, chip_at(pz, dy, dx), which)
        group = SPREAD if kind == "a" else POLICY
        launch(group, ref, ref, z_recv.at[q, 0], z_mate(1))

    def z_in(q, t, count):
        await_bytes(some_rows(count), z_recv.at[q, plane(t)])

    def chain_start(kind, q, t):
        zz = plane(t)
        ref = part(kind, chip_at(zz, 0, 0))

        def to(device):
            remote(ref, ref, sent_sem.at[CHAIN], z_recv.at[q, zz], device).start()

        pl.when(jnp.logical_and(zz <= pz, pz < PLANES - 1))(lambda: to((me + 8) % n))
        pl.when(jnp.logical_and(zz >= pz, pz > 0))(lambda: to((me + n - 8) % n))

    def far_start(kind, q):
        ref = part(kind, chip)
        remote(ref, ref, sent_sem.at[CHAIN], z_recv.at[q, pz], z_mate(3)).start()

    def chain_wait(*ts):
        for t in ts:
            z_in(2, t, rows)
            z_in(4, t, rows)

    for j in range(2, len(pieces)):
        load(j)
    for j, key in enumerate(pieces):
        where = columns(*key)
        launch(TOKENS, tokens.at[:, where], tok.at[core, :, where], tok_sem.at[j], mate)
    for a in range(3):
        pltpu.make_async_copy(params[a].at[:, mine], par.at[a, core], own_sem.at[1]).start()
        launch(SWAP, params[a].at[:, theirs], par.at[a, core], own_sem.at[1], mate)

    await_bytes(anc_send, anc_sem.at[2])
    z_out("a", 1, chip)
    spread("a", 0, pz)

    await_bytes(cot, own_sem.at[0])
    for r in range(2):
        cot_t[:, r * tokens_own : (r + 1) * tokens_own] = (
            cot[r].astype(jnp.float32).T.astype(jnp.bfloat16)
        )

    def first(key):
        await_bytes(tok.at[:, :, columns(*key)], tok_sem.at[pieces.index(key)])

    def block_gradient(i, dy, dx):
        target = chip_at(plane(3 - i), dy, dx)
        where = pl.ds(pl.multiple_of(target * block, block), block)
        total = jnp.dot(
            cot_t[:, :tokens_own], tok[0, :, where], preferred_element_type=jnp.float32
        )
        total += jnp.dot(
            cot_t[:, tokens_own:], tok[1, :, where], preferred_element_type=jnp.float32
        )
        if dx == 1:
            send_a1[i, dy] = total[:low].astype(jnp.bfloat16)
        else:
            keep_a[i, dy] = total[:low]
        if dy == 1:
            send_b1[i, dx] = total[low:].astype(jnp.bfloat16)
        else:
            keep_b[i, dx] = total[low:]

    def send_b(*at):
        launch(REDUCE, send_b1.at[at], recv_b1.at[at], rs_recv.at[1, at[0]], y_mate)

    def send_a(*at):
        launch(REDUCE, send_a1.at[at], recv_a1.at[at], rs_recv.at[0, at[0]], x_mate)

    def stage_one(i, hold=False):
        first((i, 1))
        block_gradient(i, 1, 1)
        if not hold:
            send_a(i, 1)
            send_b(i, 1)
        block_gradient(i, 1, 0)
        if not hold:
            send_b(i, 0)
        first((i, 0))
        block_gradient(i, 0, 1)
        if not hold:
            send_a(i, 0)
        block_gradient(i, 0, 0)

    def stage_two(i):
        await_bytes(recv_a1.at[i], rs_recv.at[0, i])
        send_a2[i] = (keep_a[i, 1] + recv_a1[i, 1].astype(jnp.float32)).astype(jnp.bfloat16)
        launch(REDUCE, send_a2.at[i], recv_a2.at[i], rs_recv.at[2, i], y_mate)
        await_bytes(recv_b1.at[i], rs_recv.at[1, i])
        send_b2[i] = (keep_b[i, 1] + recv_b1[i, 1].astype(jnp.float32)).astype(jnp.bfloat16)
        launch(REDUCE, send_b2.at[i], recv_b2.at[i], rs_recv.at[3, i], x_mate)

    def stage_three(i):
        await_bytes(recv_a2.at[i], rs_recv.at[2, i])
        total_a = keep_a[i, 0] + recv_a1[i, 0].astype(jnp.float32) + recv_a2[i].astype(jnp.float32)
        await_bytes(recv_b2.at[i], rs_recv.at[3, i])
        total_b = keep_b[i, 0] + recv_b1[i, 0].astype(jnp.float32) + recv_b2[i].astype(jnp.float32)
        if i == PLANES - 1:
            grad_own[:low] = total_a
            grad_own[low:] = total_b
        else:
            send_z[i, :low] = total_a.astype(jnp.bfloat16)
            send_z[i, low:] = total_b.astype(jnp.bfloat16)
            launch(REDUCE, send_z.at[i], recv_z.at[pz], rs_recv.at[4, 0], z_mate(3 - i))

    def anchor_spread(t):
        z_in(1, t, block)
        spread("a", t, plane(t))

    def anchor_relay(t):
        relay("a", t, plane(t))

    stage_one(0)
    stage_one(1)
    stage_one(2, hold=True)
    stage_two(0)
    send_b(2)
    send_a(2)
    await_bytes(some_rows(2 * block, 1), xy_recv.at[0, 0])
    beside("a", 0, 0, 1)
    beside("a", 0, 1, 0, 0)
    stage_one(3, hold=True)
    stage_two(1)
    stage_three(0)
    forward("a", 0, pz)
    stage_two(2)
    send_b(3)
    send_a(3)
    stage_three(1)
    anchor_spread(2)
    stage_three(2)
    beside("a", 0, 1, 0, 1)
    relayed("a", 0)
    beside("a", 0, 1, 1)
    stage_two(3)
    anchor_relay(2)
    await_bytes(par, own_sem.at[1])
    await_bytes(recv_z.at[pl.ds(0, PLANES - 1)], rs_recv.at[4, 0])
    stage_three(3)
    gradient = grad_own[...]
    for t in (1, 2, 3):
        gradient += recv_z[plane(t)].astype(jnp.float32)
    gradient = gradient.T
    for r in range(2):
        own = gradient[r * rows : (r + 1) * rows]
        updated = policy_update(own, par[0, r], par[1, r], par[2, r])
        result[r] = own
        weights[0, pl.ds(pl.multiple_of(home + r * rows, rows), rows), :] = updated.astype(
            jnp.bfloat16
        )
    chain_start("u", 2, 0)
    chain_start("v", 4, 0)

    @pl.when(jnp.logical_not(middle))
    def _():
        far_start("u", 2)
        far_start("v", 4)

    spread("u", 4, pz)
    spread("v", 7, pz)

    tile = tokens_own
    scale = readout[core] * LOG2E
    blend_scale = scale * blend_rate
    anchor_scale = scale * (1.0 - blend_rate)

    def score_sum(values):
        low_part = jnp.minimum(values, 0.0).reshape(LEN // 8, 8, half)
        factor = (1.0 + jnp.exp2(-jnp.abs(values))).reshape(LEN // 8, 8, half)
        product = factor[0]
        for j in range(1, LEN // 8):
            product = product * factor[j]
        return jnp.sum(low_part, axis=0) - jnp.log2(product)

    def multiply(m, zz, t):
        where = pl.ds(pl.multiple_of(zz * span, span), span)

        @pl.loop(0, 2)
        def _(i):
            value = jnp.dot(
                tok[i, :, where], weights[m, where, :], preferred_element_type=jnp.float32
            )
            value = value if t == 0 else acc[m, i] + value
            acc[m, i] = value * anchor_scale if m == 1 and t == PLANES - 1 else value

    def anchor_multiply(t):
        if t == 1:
            z_in(1, 1, block)
            await_bytes(some_rows(3 * block), z_recv.at[0, 0])
        elif t > 1:
            relayed("a", t)
        multiply(1, plane(t), t)

    first_plane = jnp.where(middle, plane(2), plane(3))
    last_plane = jnp.where(middle, plane(3), plane(2))

    def spot(zz, dy, dx):
        return pl.ds(pl.multiple_of(chip_at(zz, dy, dx) * block, block), block)

    def compute_near(zz):
        @pl.loop(0, 2)
        def _(i):
            value = acc[0, i]
            for dy, dx in ((0, 0), (0, 1), (1, 0)):
                where = spot(zz, dy, dx)
                value += jnp.dot(
                    tok[i, :, where], weights[0, where, :], preferred_element_type=jnp.float32
                )
            acc[0, i] = value

    def compute_last(zz):
        where = spot(zz, 1, 1)

        @pl.loop(0, 2)
        def _(i):
            value = acc[0, i] + jnp.dot(
                tok[i, :, where], weights[0, where, :], preferred_element_type=jnp.float32
            )
            acc[1, i] = value * blend_scale + acc[1, i]
            acc[0, i] = value * scale
            for j in range(tile // LEN):
                gap = score_sum(acc[0, i, j * LEN : (j + 1) * LEN]) - score_sum(
                    acc[1, i, j * LEN : (j + 1) * LEN]
                )
                gap = jnp.sum(gap, axis=0, keepdims=True)
                gap = jnp.sum(gap, axis=1, keepdims=True)
                table[me, pl.ds(i * (tile // LEN) + j, 1), :] = jnp.broadcast_to(
                    gap * (1.0 / (LEN * LOG2E)), (1, 128)
                )

    pltpu.make_async_copy(result.at[core], gradient_out.at[:, mine], out_sem.at[0]).start()
    launch(REDUCE, result.at[1 - core], gradient_out.at[:, mine], out_sem.at[0], mate)

    anchor_spread(3)
    anchor_multiply(0)
    for kind, q, chain_q in (("u", 4, 2), ("v", 7, 4)):
        relay(kind, q, pz)

        @pl.when(middle)
        def _():
            for t in (1, 2):
                z_in(chain_q, t, rows)
                chain_start(kind, chain_q, t)

    beside("p", 3, 0, 1)
    beside("p", 3, 1, 0)
    anchor_multiply(2)
    anchor_relay(3)
    pl.when(jnp.logical_not(middle))(lambda: chain_wait(3))
    spread("p", 5, first_plane)
    relayed("u", 4)
    relayed("v", 7)
    beside("p", 3, 1, 1)
    multiply(0, pz, 0)

    pl.when(middle)(lambda: chain_wait(3))
    pl.when(jnp.logical_not(middle))(lambda: chain_wait(2))

    spread("p", 6, last_plane)
    anchor_multiply(1)
    relay("p", 5, first_plane)
    anchor_multiply(3)
    relay("p", 6, last_plane)
    compute_near(last_plane)
    relayed("p", 5)
    multiply(0, first_plane, 2)
    pl.when(jnp.logical_not(middle))(lambda: chain_wait(1))
    await_bytes(some_rows(3 * block), z_recv.at[3, 0])
    multiply(0, plane(1), 1)
    await_bytes(gradient_out, out_sem.at[0])
    await_bytes(tok.at[0], sent_sem.at[TOKENS])
    for group in (SWAP, REDUCE, SPREAD, POLICY):
        await_bytes(some_rows(sent[group]), sent_sem.at[group])
    pl.when(middle)(lambda: await_bytes(some_rows(4 * block), sent_sem.at[CHAIN]))
    pl.when(jnp.logical_not(middle))(lambda: await_bytes(some_rows(2 * block), sent_sem.at[CHAIN]))
    relayed("p", 6)
    compute_last(last_plane)

    everyone = [
        (t, dy, dx, dc) for t in (3, 2, 1, 0) for dy, dx, dc in itertools.product((1, 0), repeat=3)
    ][:-1]
    for t, dy, dx, dc in everyone:
        there = chip_at(plane(t), dy, dx) * 2 + (core + dc) % 2
        ref = table.at[me]
        remote(ref, ref, sent_sem.at[MARGIN], out_sem.at[1], there).start()
    await_bytes(table.at[pl.ds(0, n - 1)], out_sem.at[1])
    await_bytes(table.at[pl.ds(0, n - 1)], sent_sem.at[MARGIN])
    margins = table[...].reshape(n // 2, 2, -1, 128)
    margins = (margins[:, 0] + margins[:, 1]).reshape(-1, 128)
    sequence = lax.broadcasted_iota(jnp.int32, margins.shape, 0)

    def margin_of(index):
        return jnp.sum(jnp.where(sequence == index, margins, 0.0), axis=0, keepdims=True)

    for p in range(noisy_flags.shape[0]):
        gap = margin_of(pair_index[p, 0]) - margin_of(pair_index[p, 1])
        gap = jnp.where(noisy_flags[p] == 1, -gap, gap)
        tail = jnp.log(1.0 + jnp.exp(-jnp.abs(gap)))
        loss = (1.0 - smoothing) * (tail - jnp.minimum(gap, 0.0)) + smoothing * (
            tail + jnp.maximum(gap, 0.0)
        )
        loss_out[p] = loss[0, 0]


def finish_kernel(
    gradient,
    policy,
    anchor,
    moment,
    second,
    loss,
    policy_out,
    anchor_out,
    moment_out,
    second_out,
    loss_out,
):
    updated = adam_update(gradient[...], policy[...], anchor[...], moment[...], second[...])
    for out, value in zip((policy_out, anchor_out, moment_out, second_out), updated):
        out[...] = value
    for p in range(loss.shape[0]):
        loss_out[p] = loss[p]


def fused_shards(n, tokens, cotangent, policy, anchor, moment, second, readout, pair_index, noisy_flags):
    tokens_own, depth = tokens.shape
    rows, channels = policy.shape
    half = channels // 2
    block = 2 * rows
    low = half // 2
    sizes = (n, rows, tokens_own, half)
    bf, f32 = jnp.bfloat16, jnp.float32
    vmem, dma = pltpu.VMEM, pltpu.SemaphoreType.DMA
    hbm = pl.BlockSpec(memory_space=pl.ANY)
    whole = pl.BlockSpec(memory_space=pltpu.VMEM)
    smem = pl.BlockSpec(memory_space=pltpu.SMEM)
    weight = jax.ShapeDtypeStruct((rows, channels), f32)
    losses = jax.ShapeDtypeStruct(noisy_flags.shape, f32)
    gradient, loss = pl.pallas_call(
        functools.partial(fused_kernel, sizes),
        out_shape=(pltpu.VMEM((rows, channels), f32), losses),
        in_specs=[hbm] * 6 + [whole] + [smem] * 2,
        out_specs=(hbm, smem),
        scratch_shapes=[
            vmem((2, tokens_own, depth), bf),
            vmem((2, tokens_own, half), bf),
            vmem((half, 2 * tokens_own), bf),
            vmem((2, rows, half), f32),
            vmem((rows, half), bf),
            vmem((3, 2, rows, half), f32),
            vmem((4, 2, low, block), bf),
            vmem((4, 2, low, block), bf),
            vmem((4, 2, low, block), f32),
            vmem((4, 2, low, block), bf),
            vmem((4, 2, low, block), bf),
            vmem((4, 2, low, block), f32),
            vmem((4, low, block), bf),
            vmem((4, low, block), bf),
            vmem((4, low, block), bf),
            vmem((4, low, block), bf),
            vmem((3, half, block), bf),
            vmem((4, half, block), bf),
            vmem((half, block), f32),
            vmem((2, rows, half), f32),
            vmem((2, depth, half), bf),
            vmem((2, 2, tokens_own, half), f32),
            vmem((n, 2 * tokens_own // LEN, 128), f32),
            dma((2,)),
            dma((8,)),
            dma((3,)),
            dma((5, 4)),
            dma((8, 2)),
            dma((5, 4)),
            dma((2,)),
            dma((7,)),
        ],
        compiler_params=pltpu.CompilerParams(
            collective_id=0, has_side_effects=True, vmem_limit_bytes=56 * 1024 * 1024
        ),
    )(
        tokens,
        cotangent,
        policy,
        anchor,
        moment,
        second,
        readout.reshape(2, 1, half),
        pair_index,
        noisy_flags,
    )
    policy_next, anchor_next, moment_next, second_next, pair_loss = pl.pallas_call(
        finish_kernel,
        out_shape=(weight,) * 4 + (losses,),
        in_specs=[whole] * 5 + [smem],
        out_specs=(whole,) * 4 + (smem,),
    )(*(pltpu.with_memory_space_constraint(x, pltpu.VMEM) for x in (gradient, policy, anchor, moment, second)), loss)
    return (policy_next, anchor_next, moment_next, second_next, pair_loss)


def solution(mesh):
    placed = (
        P(("rep", "fsdp"), None),
        P(("rep", "fsdp"), None),
        P("fsdp", None),
        P("fsdp", None),
        P("fsdp", None),
        P("fsdp", None),
        P(),
        P(("rep", "fsdp"), None),
        P(("rep", "fsdp")),
    )
    n = mesh.shape["fsdp"]
    body = shards
    if mesh.shape["rep"] == 1 and n == 8 * PLANES:
        body = functools.partial(fused_shards, n)
    return jax.shard_map(
        body,
        mesh=mesh,
        in_specs=placed,
        out_specs=(
            P("fsdp", None),
            P("fsdp", None),
            P("fsdp", None),
            P("fsdp", None),
            P(("rep", "fsdp")),
        ),
        check_vma=False,
    )
```
